32 devices in a mesh: tm: 2 (over core), space: 16 (over z, y, x).
Axes of the slice: x: 2, y: 2, z: 4, core: 2. Of those that a mesh axis runs over, the one named last changes fastest.
Arguments:
- slab_starts: float32 [2, 64, 24, 512], P('tm', 'space'), may hold values from -6 to 6
- forcing: float32 [2, 2, 64, 24, 512], P('tm', None, 'space'), may hold values from -5 to 5
- density: float32 [64, 24, 512], P('space'), may hold values from 0.25 to 4
- moving_flags: int32 [64, 24, 512], P('space'), may hold values 0 or 1
Outputs:
- new_starts: float32 [2, 64, 24, 512], P('tm', 'space')
- new_interior: float32 [2, 64, 24, 512], P('tm', 'space')
The draws below stay inside these ranges and needn't reach their ends.
All inputs are finite; a program needn't handle non-finite values. No bound on the sum of `moving_flags` on one device may be relied on, other than what follows from the above.
Results may differ from the reference program's by a relative error of at most 0.0001.
Values sent between devices are 32-bit elements; how exact they have to be, the bound alone decides.
A program may use at most 64 MiB of HBM per device.

```python
import math
import jax
import jax.numpy as jnp
from jax import lax

NY = 24
NZ = 512
STEPS = 2
VCYCLES = 1
COARSE_SWEEPS = 4
SLABS = 2
NX = 64


def draw_forcing(key, part):
    shape = (SLABS, STEPS, NX, NY, NZ)
    values = jnp.clip(jax.random.normal(key, shape, jnp.float32), -5.0, 5.0)
    return values


def plant(result, key, low, top_value):
    spot = [jax.random.randint(jax.random.fold_in(key, axis), (), 0, length) for axis, length in enumerate(result.shape)]
    main_axis = result.shape.index(max(result.shape))
    next_to = spot[:main_axis] + [(spot[main_axis] + 1) % result.shape[main_axis]] + spot[main_axis + 1:]
    return result.at[tuple(spot)].set(low).at[tuple(next_to)].set(top_value)


def block_scale(rng, dims, pieces, smallest, largest):
    gain, own = 1.0, jax.random.fold_in(rng, 6)
    for dim, parts in pieces:
        steps = jnp.exp(jax.random.uniform(jax.random.fold_in(own, dim), (parts,), jnp.float32, smallest / len(pieces), largest / len(pieces)))
        gain = gain * jnp.repeat(steps, dims[dim] // parts).reshape([-1 if axis == dim else 1 for axis in range(len(dims))])
    return gain


def gaussian(stream_key, dims, scale, limit, shards=(), held_as=jnp.bfloat16):
    array = jax.random.normal(stream_key, dims, jnp.float32) * scale
    if len(shards) > 0:
        array = block_scale(stream_key, dims, shards, -0.22, 0.18) * array
    return jnp.clip(array, min=-limit, max=limit).astype(held_as)


def setup_inputs(seed: int = 0) -> dict:
    key_of = jax.random.split(jax.random.key(seed), 5)
    slab_starts = gaussian(key_of[0], (SLABS, NX, NY, NZ), 1.0, 6.0, ((0, 2), (1, 16)), jnp.float32)
    forcing = draw_forcing(jax.random.fold_in(key_of[4], 71), 0)
    density = jnp.clip(jnp.exp(math.log(4.0) - 2.7725887 * jax.random.uniform(key_of[2], (NX, NY, NZ), jnp.float32) ** block_scale(key_of[2], (NX, NY, NZ), ((0, 16),), -0.2, 0.2)), 0.25, 4.0)
    moving_flags = plant((jax.random.randint(key_of[3], (NX, NY, NZ), 0, 4) < 1).astype(jnp.int32), jax.random.fold_in(key_of[3], 1), 0, 1)
    return dict(slab_starts=slab_starts, forcing=forcing, density=density, moving_flags=moving_flags)


STIFFNESS = 4.0
COARSE_STIFF = 0.25
FORCE_WEIGHT = 0.5
RELAX = 0.8
MASS_FLAG = 3.0


def shrink(field):
    a, b, c = field.shape
    return field.reshape(a // 2, 2, b // 2, 2, c // 2, 2).mean(axis=(1, 3, 5))


def expand(field):
    return jnp.repeat(jnp.repeat(jnp.repeat(field, 2, axis=0), 2, axis=1), 2, axis=2)


def neighbour_sum(field):
    padded = jnp.pad(field, 1)
    total = padded[2:, 1:-1, 1:-1] + padded[:-2, 1:-1, 1:-1]
    total = total + padded[1:-1, 2:, 1:-1] + padded[1:-1, :-2, 1:-1]
    return total + padded[1:-1, 1:-1, 2:] + padded[1:-1, 1:-1, :-2]


def operate(field, mass, conduct, stiff):
    return mass * field + stiff * conduct * (6.0 * field - neighbour_sum(field))


def advance(prior, source, mass, conduct, mass_c, conduct_c):
    rhs = mass * prior + FORCE_WEIGHT * source
    diag = mass + 6.0 * STIFFNESS * conduct
    diag_c = mass_c + 6.0 * COARSE_STIFF * conduct_c
    state = prior
    for cycle in range(VCYCLES):
        state = state + RELAX * (rhs - operate(state, mass, conduct, STIFFNESS)) / diag
        resid = rhs - operate(state, mass, conduct, STIFFNESS)
        coarse_rhs = shrink(shrink(resid))
        error = RELAX * coarse_rhs / diag_c
        for sweep in range(COARSE_SWEEPS - 1):
            error = error + RELAX * (coarse_rhs - operate(error, mass_c, conduct_c, COARSE_STIFF)) / diag_c
        state = state + expand(expand(error))
    return state


def reference(slab_starts, forcing, density, moving_flags):
    conduct = 1.0 / density
    mass = 1.0 + MASS_FLAG * moving_flags.astype(jnp.float32)
    mass_c = shrink(shrink(mass))
    conduct_c = shrink(shrink(conduct))

    def whole_slab(pair):
        start, source = pair
        middle = advance(start, source[0], mass, conduct, mass_c, conduct_c)
        return advance(middle, source[1], mass, conduct, mass_c, conduct_c)

    ends = lax.map(whole_slab, (slab_starts, forcing))
    new_starts = jnp.roll(ends, 1, axis=0)

    def first_step(pair):
        return advance(pair[0], pair[1][0], mass, conduct, mass_c, conduct_c)

    new_interior = lax.map(first_step, (new_starts, forcing))
    return (new_starts, new_interior)
```

```python
import functools

import jax
import jax.numpy as jnp
from jax import lax
from jax.experimental import pallas as pl
from jax.experimental.pallas import tpu as pltpu
from jax.sharding import PartitionSpec as P

COARSE_SWEEPS = 4
STIFFNESS = 4.0
COARSE_STIFF = 0.25
FORCE_WEIGHT = 0.5
RELAX = 0.8
MASS_FLAG = 3.0

MESH = pl.DeviceIdType.MESH
REACH = COARSE_SWEEPS
SLOTS = 2 * REACH + 1
F32 = jnp.float32
BF16 = jnp.bfloat16


def pieces(x):
    hi = x.astype(BF16).astype(F32)
    rest = x - hi
    mid = rest.astype(BF16).astype(F32)
    low = (rest - mid).astype(BF16).astype(F32)
    return [hi, mid, low]


def kernel(
    n, nt, planes,
    starts, forcing, density, flags, out_starts, out_interior,
    prior, state, came, force, rho, moving, stiff, diag, beta,
    ring, own, gam, rows, wide, narrow, spread, final,
    load_sem, send_sem, recv_sem,
):
    t = lax.axis_index("tm")
    me = lax.axis_index("space")
    ahead, behind = lax.rem(t + 1, nt), lax.rem(t + nt - 1, nt)
    top = planes + 1
    ny, nz = prior.shape[-2:]
    ncy, ncz = 8, nz // 4

    def inside(offset):
        if offset < 0:
            return me >= -offset
        return me < n - offset

    offsets = [d for d in range(-REACH, REACH + 1)]

    barrier = pltpu.get_barrier_semaphore()
    for d in (1, -1, 2, -2, 3, -3, 4, -4):
        @pl.when(inside(d))
        def _(d=d):
            pl.semaphore_signal(barrier, inc=1, device_id=(t, me + d), device_id_type=MESH)
            pl.semaphore_signal(barrier, inc=1, device_id=(behind, me + d), device_id_type=MESH)
    pl.semaphore_signal(barrier, inc=1, device_id=(behind, me), device_id_type=MESH)

    loads = [
        pltpu.make_async_copy(density, rho, load_sem.at[0]),
        pltpu.make_async_copy(flags, moving, load_sem.at[1]),
        pltpu.make_async_copy(starts.at[0], prior.at[0, pl.ds(1, planes)], load_sem.at[2]),
        pltpu.make_async_copy(forcing.at[0], force, load_sem.at[3]),
    ]
    for load in loads:
        load.start()

    sends = []

    def copy_to(src, dst, k, device):
        return pltpu.make_async_remote_copy(
            src_ref=src, dst_ref=dst, send_sem=send_sem.at[k], recv_sem=recv_sem.at[k],
            device_id=device, device_id_type=MESH,
        )

    def send(src, dst, k, offset, tm):
        copy = copy_to(src, dst, k, (tm, me + offset))
        if offset == 0:
            copy.start()
        else:
            pl.when(inside(offset))(lambda: copy.start())
        sends.append((copy, offset))

    def receive(dst, k, offset):
        copy = copy_to(dst, dst, k, (t, me))
        if offset == 0:
            copy.wait_recv()
        else:
            pl.when(inside(offset))(lambda: copy.wait_recv())

    for d in offsets:
        if d == 0:
            continue

        @pl.when(jnp.logical_not(inside(d)))
        def _(d=d):
            zero = jnp.zeros(ring.shape[2:], F32)
            gam[REACH + d] = zero
            for step in range(3):
                ring[step, REACH + d] = zero
            if abs(d) == 1:
                plane = 0 if d < 0 else top
                fine_zero = jnp.zeros((ny, nz), F32)
                prior[0, plane] = fine_zero
                for step in range(3):
                    state[step, plane] = fine_zero

    narrow[...] = (
        lax.broadcasted_iota(jnp.int32, (nz, ncz), 0) // 4 == lax.broadcasted_iota(jnp.int32, (nz, ncz), 1)
    ).astype(F32).astype(BF16)
    one = (
        lax.broadcasted_iota(jnp.int32, (ncz, nz), 1) // 4 == lax.broadcasted_iota(jnp.int32, (ncz, nz), 0)
    ).astype(F32).astype(BF16)
    for piece in range(3):
        wide[pl.ds(piece * ncz, ncz), :] = one
    rows[...] = jnp.zeros_like(rows)

    row = lax.broadcasted_iota(jnp.int32, (ny, nz), 0)
    lane = lax.broadcasted_iota(jnp.int32, (ny, nz), 1)

    def beside(x):
        up = jnp.where(row == 0, 0.0, pltpu.roll(x, 1, 0))
        down = jnp.where(row == ny - 1, 0.0, pltpu.roll(x, ny - 1, 0))
        left = jnp.where(lane == 0, 0.0, pltpu.roll(x, 1, 1))
        right = jnp.where(lane == nz - 1, 0.0, pltpu.roll(x, nz - 1, 1))
        return (up + down) + (left + right)

    clane = lax.broadcasted_iota(jnp.int32, (ncy, ncz), 1)

    def coarse_beside(x):
        left = jnp.where(clane == 0, 0.0, pltpu.roll(x, 1, 1))
        right = jnp.where(clane == ncz - 1, 0.0, pltpu.roll(x, ncz - 1, 1))
        return (pltpu.roll(x, 1, 0) + pltpu.roll(x, ncy - 1, 0)) + (left + right)

    def coarsen(total, slot):
        stacked = jnp.concatenate(pieces(total), axis=0).astype(BF16)
        product = jnp.dot(stacked, narrow[...], preferred_element_type=F32)
        rows[slot, pl.ds(0, ny), :] = (product[:ny] + product[ny:2 * ny]) + product[2 * ny:]
        parts = [rows[slot, pl.ds(k, ncy, stride=4), :] for k in range(4)]
        return ((parts[0] + parts[1]) + (parts[2] + parts[3])) * (1.0 / 64.0)

    for load in loads[:2]:
        load.wait()
    mass_sum = jnp.zeros((ny, nz), F32)
    conduct_sum = jnp.zeros((ny, nz), F32)
    for k in range(planes):
        conduct = 1.0 / rho[k]
        mass = 1.0 + MASS_FLAG * moving[k].astype(F32)
        full = mass + 6.0 * STIFFNESS * conduct
        stiff[k] = STIFFNESS * conduct
        diag[k] = full
        beta[k] = RELAX / full
        mass_sum = mass_sum + mass
        conduct_sum = conduct_sum + conduct

    pl.semaphore_wait(barrier, 1 + 2 * sum(inside(d).astype(jnp.int32) for d in offsets if d != 0))
    send(starts.at[0, 0], prior.at[0, top], 1, -1, t)
    send(starts.at[0, planes - 1], prior.at[0, 0], 0, 1, t)

    mass_c = coarsen(mass_sum, 0)
    conduct_c = coarsen(conduct_sum, 1)
    real = lax.broadcasted_iota(jnp.int32, (ncy, ncz), 0) < ny // 4
    relax_c = jnp.where(real, RELAX / jnp.where(real, mass_c + 6.0 * COARSE_STIFF * conduct_c, 1.0), 0.0)
    gam[REACH] = COARSE_STIFF * conduct_c * relax_c
    for d in offsets:
        if d != 0:
            send(gam.at[REACH], gam.at[REACH - d], 20 + REACH - d, d, t)
    for load in loads[2:]:
        load.wait()

    def smooth(step, k):
        source = force[step % 2, k]
        here = prior[step, k + 1]
        around = beside(here) + (prior[step, k] + prior[step, k + 2])
        state[step, k + 1] = here + beta[k] * (FORCE_WEIGHT * source - stiff[k] * (6.0 * here - around))

    def residual(step):
        total = jnp.zeros((ny, nz), F32)
        for k in range(planes):
            full, mine = diag[k], state[step, k + 1]
            mass = full - 6.0 * stiff[k]
            around = beside(mine)
            if k > 0:
                around = around + state[step, k]
            if k < planes - 1:
                around = around + state[step, k + 2]
            total = total + (mass * prior[step, k + 1] + FORCE_WEIGHT * force[step % 2, k]) - (full * mine - stiff[k] * around)
        return total

    def solve(step, width):
        right = {i: ring[step, i] for i in range(1 - width, SLOTS - 1 + width)}
        error = right
        for sweep in range(COARSE_SWEEPS - 1):
            reach = COARSE_SWEEPS - 2 - sweep + width
            error = {
                i: (1.0 - RELAX) * error[i] + right[i]
                + gam[i] * (coarse_beside(error[i]) + (error[i - 1] + error[i + 1]))
                for i in range(REACH - reach, REACH + reach + 1)
            }
        return [error[i] for i in range(REACH - width, REACH + width + 1)]

    def expanded(errors):
        for j, error in enumerate(errors):
            for k in range(4):
                spread[j, pl.ds(k, ncy, stride=4), :] = error
        tall = jnp.concatenate([spread[j, pl.ds(0, ny), :] for j in range(len(errors))], axis=0)
        stacked = jnp.concatenate(pieces(tall), axis=1).astype(BF16)
        product = jnp.dot(stacked, wide[...], preferred_element_type=F32)
        return [product[j * ny:(j + 1) * ny] for j in range(len(errors))]

    def exchange(step):
        send(state.at[step, 1], state.at[step, top], 3 + 2 * step, -1, t)

    for step in range(3):
        low, high = 2 + 2 * step, 3 + 2 * step
        if step == 0:
            for k in range(1, planes - 1):
                smooth(step, k)
            receive(prior.at[0, 0], 0, -1)
            smooth(step, 0)
            send(state.at[step, 1], state.at[step, top], high, -1, t)
            receive(prior.at[0, top], 1, 1)
            smooth(step, planes - 1)
            send(state.at[step, planes], state.at[step, 0], low, 1, t)
        else:
            smooth(step, 0)
            send(state.at[step, 1], state.at[step, top], high, -1, t)
            smooth(step, planes - 1)
            send(state.at[step, planes], state.at[step, 0], low, 1, t)
            for k in range(1, planes - 1):
                smooth(step, k)
        if step == 1:
            send(state.at[step, pl.ds(1, planes)], came.at[pl.ds(1, planes)], 8, 0, ahead)
        total = residual(step)
        receive(state.at[step, 0], low, -1)
        receive(state.at[step, top], high, 1)
        total = total + stiff[0] * state[step, 0] + stiff[planes - 1] * state[step, top]
        right = relax_c * coarsen(total, step % 2)
        if step == 1:
            own[...] = right
            for d in offsets:
                send(own, ring.at[step, REACH - d], 40 + REACH - d, d, ahead)
            send(state.at[step, 0], came.at[0], 9, 0, ahead)
            send(state.at[step, top], came.at[top], 10, 0, ahead)
        else:
            ring[step, REACH] = right
            for d in offsets:
                if d != 0 and (step == 0 or abs(d) < REACH):
                    send(ring.at[step, REACH], ring.at[step, REACH - d], 30 + 10 * step + REACH - d, d, t)
        if step == 0:
            for d in offsets:
                if d != 0:
                    receive(gam.at[REACH + d], 20 + REACH + d, d)
        for d in offsets:
            if (d != 0 or step == 1) and (step < 2 or abs(d) < REACH):
                receive(ring.at[step, REACH + d], 30 + 10 * step + REACH + d, d)
        if step < 2:
            corrections = expanded(solve(step, 1))
            if step == 1:
                receive(came.at[pl.ds(1, planes)], 8, 0)
                receive(came.at[0], 9, 0)
                receive(came.at[top], 10, 0)
            for k in range(planes + 2):
                which = 0 if k == 0 else 2 if k == top else 1
                base = state[0, k] if step == 0 else came[k]
                prior[step + 1, k] = base + corrections[which]
            if step == 1:
                done = pltpu.make_async_copy(prior.at[2, pl.ds(1, planes)], out_starts.at[0], load_sem.at[4])
                done.start()
        else:
            correction = expanded(solve(step, 0))[0]
            for k in range(planes):
                final[k] = state[2, k + 1] + correction
    last = pltpu.make_async_copy(final, out_interior.at[0], load_sem.at[5])
    last.start()
    for copy, offset in sends:
        if offset == 0:
            copy.wait_send()
        else:
            pl.when(inside(offset))(lambda copy=copy: copy.wait_send())
    done.wait()
    last.wait()


def solution(mesh):
    n, nt = mesh.shape["space"], mesh.shape["tm"]

    def local(slab_starts, forcing, density, moving_flags):
        _, planes, ny, nz = slab_starts.shape
        block = (planes, ny, nz)
        coarse = (8, nz // 4)
        result = jax.ShapeDtypeStruct(slab_starts.shape, F32)
        return pl.pallas_call(
            functools.partial(kernel, n, nt, planes),
            out_shape=(result, result),
            in_specs=[pl.BlockSpec(memory_space=pl.ANY)] * 4,
            out_specs=(pl.BlockSpec(memory_space=pl.ANY),) * 2,
            scratch_shapes=[
                pltpu.VMEM((3, planes + 2, ny, nz), F32),
                pltpu.VMEM((3, planes + 2, ny, nz), F32),
                pltpu.VMEM((planes + 2, ny, nz), F32),
                pltpu.VMEM((2,) + block, F32),
                pltpu.VMEM(block, F32),
                pltpu.VMEM(block, jnp.int32),
                pltpu.VMEM(block, F32),
                pltpu.VMEM(block, F32),
                pltpu.VMEM(block, F32),
                pltpu.VMEM((3, SLOTS) + coarse, F32),
                pltpu.VMEM(coarse, F32),
                pltpu.VMEM((SLOTS,) + coarse, F32),
                pltpu.VMEM((2, 32, nz // 4), F32),
                pltpu.VMEM((3 * nz // 4, nz), BF16),
                pltpu.VMEM((nz, nz // 4), BF16),
                pltpu.VMEM((3, 32, nz // 4), F32),
                pltpu.VMEM(block, F32),
                pltpu.SemaphoreType.DMA((6,)),
                pltpu.SemaphoreType.DMA((60,)),
                pltpu.SemaphoreType.DMA((60,)),
            ],
            compiler_params=pltpu.CompilerParams(
                collective_id=0, has_side_effects=True, vmem_limit_bytes=32 * 1024 * 1024
            ),
            name="cycle",
        )(slab_starts, forcing, density, moving_flags)

    placed = (
        P("tm", "space", None, None),
        P("tm", None, "space", None, None),
        P("space", None, None),
        P("space", None, None),
    )
    return jax.shard_map(
        local,
        mesh=mesh,
        in_specs=placed,
        out_specs=(P("tm", "space", None, None), P("tm", "space", None, None)),
        check_vma=False,
    )
```

```python
import functools

import jax
import jax.numpy as jnp
from jax import lax
from jax.experimental import pallas as pl
from jax.experimental.pallas import tpu as pltpu
from jax.sharding import PartitionSpec as P

COARSE_SWEEPS = 4
STIFFNESS = 4.0
COARSE_STIFF = 0.25
FORCE_WEIGHT = 0.5
RELAX = 0.8
MASS_FLAG = 3.0

MESH = pl.DeviceIdType.MESH
REACH = COARSE_SWEEPS
SLOTS = 2 * REACH + 1
F32 = jnp.float32
BF16 = jnp.bfloat16


def pieces(x):
    hi = x.astype(BF16).astype(F32)
    rest = x - hi
    mid = rest.astype(BF16).astype(F32)
    low = (rest - mid).astype(BF16).astype(F32)
    return [hi, mid, low]


def kernel(
    n, nt, planes,
    starts, forcing, density, flags, out_starts, out_interior,
    prior, state, came, force, rho, moving, stiff, diag, alpha, beta, local_part,
    ring, own, gam, rows, wide, narrow, spread, final,
    load_sem, send_sem, recv_sem,
):
    t = lax.axis_index("tm")
    me = lax.axis_index("space")
    ahead, behind = lax.rem(t + 1, nt), lax.rem(t + nt - 1, nt)
    top = planes + 2
    ny, nz = prior.shape[-2:]
    ncy, ncz = 8, nz // 4

    def inside(offset):
        if offset < 0:
            return me >= -offset
        return me < n - offset

    offsets = [d for d in range(-REACH, REACH + 1)]

    barrier = pltpu.get_barrier_semaphore()
    for d in (1, -1, 2, -2, 3, -3, 4, -4):
        @pl.when(inside(d))
        def _(d=d):
            pl.semaphore_signal(barrier, inc=1, device_id=(t, me + d), device_id_type=MESH)
            pl.semaphore_signal(barrier, inc=1, device_id=(behind, me + d), device_id_type=MESH)
    pl.semaphore_signal(barrier, inc=1, device_id=(behind, me), device_id_type=MESH)

    loads = [
        pltpu.make_async_copy(density, rho, load_sem.at[0]),
        pltpu.make_async_copy(flags, moving, load_sem.at[1]),
        pltpu.make_async_copy(starts.at[0], prior.at[0, pl.ds(2, planes)], load_sem.at[2]),
        pltpu.make_async_copy(forcing.at[0], force, load_sem.at[3]),
    ]
    for load in loads:
        load.start()

    sends = []

    def copy_to(src, dst, k, device):
        return pltpu.make_async_remote_copy(
            src_ref=src, dst_ref=dst, send_sem=send_sem.at[k], recv_sem=recv_sem.at[k],
            device_id=device, device_id_type=MESH,
        )

    def send(src, dst, k, offset, tm):
        copy = copy_to(src, dst, k, (tm, me + offset))
        if offset == 0:
            copy.start()
        else:
            pl.when(inside(offset))(lambda: copy.start())
        sends.append((copy, offset))

    def receive(dst, k, offset):
        copy = copy_to(dst, dst, k, (t, me))
        if offset == 0:
            copy.wait_recv()
        else:
            pl.when(inside(offset))(lambda: copy.wait_recv())

    for d in offsets:
        if d == 0:
            continue

        @pl.when(jnp.logical_not(inside(d)))
        def _(d=d):
            zero = jnp.zeros(ring.shape[2:], F32)
            gam[REACH + d] = zero
            for step in range(3):
                ring[step, REACH + d] = zero
            if abs(d) == 1:
                side = 0 if d < 0 else 1
                fine_zero = jnp.zeros((ny, nz), F32)
                prior[0, 1 if d < 0 else top] = fine_zero
                local_part[side] = fine_zero
                beta[side * (planes + 1)] = fine_zero
                alpha[0, side * (planes + 1)] = fine_zero
                alpha[1, side * (planes + 1)] = fine_zero
                state[0, side * (top + 1)] = fine_zero
                came[side * (top + 1)] = fine_zero

    narrow[...] = (
        lax.broadcasted_iota(jnp.int32, (nz, ncz), 0) // 4 == lax.broadcasted_iota(jnp.int32, (nz, ncz), 1)
    ).astype(F32).astype(BF16)
    one = (
        lax.broadcasted_iota(jnp.int32, (ncz, nz), 1) // 4 == lax.broadcasted_iota(jnp.int32, (ncz, nz), 0)
    ).astype(F32).astype(BF16)
    for piece in range(3):
        wide[pl.ds(piece * ncz, ncz), :] = one
    rows[...] = jnp.zeros_like(rows)

    row = lax.broadcasted_iota(jnp.int32, (ny, nz), 0)
    lane = lax.broadcasted_iota(jnp.int32, (ny, nz), 1)

    def beside(x):
        up = jnp.where(row == 0, 0.0, pltpu.roll(x, 1, 0))
        down = jnp.where(row == ny - 1, 0.0, pltpu.roll(x, ny - 1, 0))
        left = jnp.where(lane == 0, 0.0, pltpu.roll(x, 1, 1))
        right = jnp.where(lane == nz - 1, 0.0, pltpu.roll(x, nz - 1, 1))
        return (up + down) + (left + right)

    clane = lax.broadcasted_iota(jnp.int32, (ncy, ncz), 1)

    def coarse_beside(x):
        left = jnp.where(clane == 0, 0.0, pltpu.roll(x, 1, 1))
        right = jnp.where(clane == ncz - 1, 0.0, pltpu.roll(x, ncz - 1, 1))
        return (pltpu.roll(x, 1, 0) + pltpu.roll(x, ncy - 1, 0)) + (left + right)

    def coarsen(total, slot):
        stacked = jnp.concatenate(pieces(total), axis=0).astype(BF16)
        product = jnp.dot(stacked, narrow[...], preferred_element_type=F32)
        rows[slot, pl.ds(0, ny), :] = (product[:ny] + product[ny:2 * ny]) + product[2 * ny:]
        parts = [rows[slot, pl.ds(k, ncy, stride=4), :] for k in range(4)]
        return ((parts[0] + parts[1]) + (parts[2] + parts[3])) * (1.0 / 64.0)

    pl.semaphore_wait(barrier, 1 + 2 * sum(inside(d).astype(jnp.int32) for d in offsets if d != 0))
    send(starts.at[0, 0], prior.at[0, top], 1, -1, t)
    send(starts.at[0, planes - 1], prior.at[0, 1], 0, 1, t)

    for load in loads:
        load.wait()

    def coefficients(k):
        conduct = 1.0 / rho[k]
        mass = 1.0 + MASS_FLAG * moving[k].astype(F32)
        full = mass + 6.0 * STIFFNESS * conduct
        relax = RELAX / full
        stiff[k] = STIFFNESS * conduct
        diag[k] = full
        beta[k + 1] = (STIFFNESS * conduct) * relax
        for step in range(2):
            alpha[step, k + 1] = (FORCE_WEIGHT * force[step, k]) * relax
        return mass, conduct

    def smooth(step, i, below=True, above=True):
        here = prior[step, i]
        around = beside(here)
        if below:
            around = around + prior[step, i - 1]
        if above:
            around = around + prior[step, i + 1]
        return here + (alpha[step % 2, i - 1] + beta[i - 1] * (around - 6.0 * here))

    sums = [coefficients(0)]
    send(beta.at[1], beta.at[planes + 1], 3, -1, t)
    part_low = smooth(0, 2, below=False)
    local_part[2] = part_low
    send(local_part.at[2], local_part.at[1], 5, -1, t)
    sums.append(coefficients(planes - 1))
    send(beta.at[planes], beta.at[0], 2, 1, t)
    part_high = smooth(0, planes + 1, above=False)
    local_part[3] = part_high
    send(local_part.at[3], local_part.at[0], 4, 1, t)
    for k in range(1, planes - 1):
        sums.append(coefficients(k))
    mass_sum = functools.reduce(lambda a, b: a + b, [m for m, _ in sums])
    conduct_sum = functools.reduce(lambda a, b: a + b, [c for _, c in sums])

    mass_c = coarsen(mass_sum, 0)
    conduct_c = coarsen(conduct_sum, 1)
    real = lax.broadcasted_iota(jnp.int32, (ncy, ncz), 0) < ny // 4
    relax_c = jnp.where(real, RELAX / jnp.where(real, mass_c + 6.0 * COARSE_STIFF * conduct_c, 1.0), 0.0)
    gam[REACH] = COARSE_STIFF * conduct_c * relax_c
    for d in offsets:
        if d != 0:
            send(gam.at[REACH], gam.at[REACH - d], 20 + REACH - d, d, t)

    def residual(step):
        total = jnp.zeros((ny, nz), F32)
        for k in range(planes):
            full, mine = diag[k], state[step, k + 2]
            mass = 1.0 + MASS_FLAG * moving[k].astype(F32)
            around = beside(mine) + (state[step, k + 1] + state[step, k + 3])
            total = total + (mass * prior[step, k + 2] + FORCE_WEIGHT * force[step % 2, k]) - (full * mine - stiff[k] * around)
        return total

    def solve(step, width):
        right = {i: ring[step, i] for i in range(1 - width, SLOTS - 1 + width)}
        error = right
        for sweep in range(COARSE_SWEEPS - 1):
            reach = COARSE_SWEEPS - 2 - sweep + width
            error = {
                i: (1.0 - RELAX) * error[i] + right[i]
                + gam[i] * (coarse_beside(error[i]) + (error[i - 1] + error[i + 1]))
                for i in range(REACH - reach, REACH + reach + 1)
            }
        return [error[i] for i in range(REACH - width, REACH + width + 1)]

    def expanded(errors):
        for j, error in enumerate(errors):
            for k in range(4):
                spread[j, pl.ds(k, ncy, stride=4), :] = error
        tall = jnp.concatenate([spread[j, pl.ds(0, ny), :] for j in range(len(errors))], axis=0)
        stacked = jnp.concatenate(pieces(tall), axis=1).astype(BF16)
        product = jnp.dot(stacked, wide[...], preferred_element_type=F32)
        return [product[j * ny:(j + 1) * ny] for j in range(len(errors))]

    for step in range(3):
        if step == 0:
            for i in range(3, planes + 1):
                state[0, i] = smooth(0, i)
            receive(prior.at[0, 1], 0, -1)
            state[0, 2] = local_part[2] + beta[1] * prior[0, 1]
            receive(prior.at[0, top], 1, 1)
            state[0, planes + 1] = local_part[3] + beta[planes] * prior[0, top]
        else:
            for i in range(3, planes + 1):
                state[step, i] = smooth(step, i)
        if step == 0:
            send(state.at[0, 3], state.at[0, top + 1], 7, -1, t)
            send(state.at[0, planes], state.at[0, 0], 6, 1, t)
        elif step == 1:
            send(state.at[1, 3], came.at[top + 1], 9, -1, ahead)
            send(state.at[1, planes], came.at[0], 8, 1, ahead)
        if step == 0:
            receive(beta.at[0], 2, -1)
            receive(local_part.at[0], 4, -1)
            state[0, 1] = local_part[0] + beta[0] * prior[0, 2]
            receive(beta.at[planes + 1], 3, 1)
            receive(local_part.at[1], 5, 1)
            state[0, top] = local_part[1] + beta[planes + 1] * prior[0, planes + 1]
        else:
            receive(alpha.at[step % 2, 0], 13 + 2 * step, -1)
            receive(alpha.at[step % 2, planes + 1], 14 + 2 * step, 1)
            for i in (1, 2, planes + 1, top):
                state[step, i] = smooth(step, i)
        if step == 1:
            send(state.at[1, pl.ds(1, planes + 2)], came.at[pl.ds(1, planes + 2)], 14, 0, ahead)
        right = relax_c * coarsen(residual(step), step % 2)
        if step == 1:
            own[...] = right
            for d in offsets:
                send(own, ring.at[step, REACH - d], 40 + REACH - d, d, ahead)
        else:
            ring[step, REACH] = right
            for d in offsets:
                if d != 0 and (step == 0 or abs(d) < REACH):
                    send(ring.at[step, REACH], ring.at[step, REACH - d], 30 + 10 * step + REACH - d, d, t)
        if step < 2:
            which = 1 - step
            send(alpha.at[which, 1], alpha.at[which, planes + 1], 16 + 2 * step, -1, t)
            send(alpha.at[which, planes], alpha.at[which, 0], 15 + 2 * step, 1, t)
        if step == 0:
            for d in offsets:
                if d != 0:
                    receive(gam.at[REACH + d], 20 + REACH + d, d)
        for d in offsets:
            if (d != 0 or step == 1) and (step < 2 or abs(d) < REACH):
                receive(ring.at[step, REACH + d], 30 + 10 * step + REACH + d, d)
        if step < 2:
            corrections = expanded(solve(step, 1))
            if step == 0:
                receive(state.at[0, 0], 6, -1)
                receive(state.at[0, top + 1], 7, 1)
            else:
                receive(came.at[0], 8, -1)
                receive(came.at[top + 1], 9, 1)
                receive(came.at[pl.ds(1, planes + 2)], 14, 0)
            for i in range(planes + 4):
                which = 0 if i < 2 else 2 if i >= top else 1
                base = state[0, i] if step == 0 else came[i]
                prior[step + 1, i] = base + corrections[which]
            if step == 1:
                done = pltpu.make_async_copy(prior.at[2, pl.ds(2, planes)], out_starts.at[0], load_sem.at[4])
                done.start()
        else:
            correction = expanded(solve(step, 0))[0]
            for k in range(planes):
                final[k] = state[2, k + 2] + correction
    last = pltpu.make_async_copy(final, out_interior.at[0], load_sem.at[5])
    last.start()
    for copy, offset in sends:
        if offset == 0:
            copy.wait_send()
        else:
            pl.when(inside(offset))(lambda copy=copy: copy.wait_send())
    done.wait()
    last.wait()


def solution(mesh):
    n, nt = mesh.shape["space"], mesh.shape["tm"]

    def local(slab_starts, forcing, density, moving_flags):
        _, planes, ny, nz = slab_starts.shape
        block = (planes, ny, nz)
        coarse = (8, nz // 4)
        result = jax.ShapeDtypeStruct(slab_starts.shape, F32)
        return pl.pallas_call(
            functools.partial(kernel, n, nt, planes),
            out_shape=(result, result),
            in_specs=[pl.BlockSpec(memory_space=pl.ANY)] * 4,
            out_specs=(pl.BlockSpec(memory_space=pl.ANY),) * 2,
            scratch_shapes=[
                pltpu.VMEM((3, planes + 4, ny, nz), F32),
                pltpu.VMEM((3, planes + 4, ny, nz), F32),
                pltpu.VMEM((planes + 4, ny, nz), F32),
                pltpu.VMEM((2,) + block, F32),
                pltpu.VMEM(block, F32),
                pltpu.VMEM(block, jnp.int32),
                pltpu.VMEM(block, F32),
                pltpu.VMEM(block, F32),
                pltpu.VMEM((2, planes + 2, ny, nz), F32),
                pltpu.VMEM((planes + 2, ny, nz), F32),
                pltpu.VMEM((4, ny, nz), F32),
                pltpu.VMEM((3, SLOTS) + coarse, F32),
                pltpu.VMEM(coarse, F32),
                pltpu.VMEM((SLOTS,) + coarse, F32),
                pltpu.VMEM((2, 32, nz // 4), F32),
                pltpu.VMEM((3 * nz // 4, nz), BF16),
                pltpu.VMEM((nz, nz // 4), BF16),
                pltpu.VMEM((3, 32, nz // 4), F32),
                pltpu.VMEM(block, F32),
                pltpu.SemaphoreType.DMA((6,)),
                pltpu.SemaphoreType.DMA((60,)),
                pltpu.SemaphoreType.DMA((60,)),
            ],
            compiler_params=pltpu.CompilerParams(
                collective_id=0, has_side_effects=True, vmem_limit_bytes=32 * 1024 * 1024
            ),
            name="cycle",
        )(*[pltpu.with_memory_space_constraint(x, pltpu.HBM) for x in (slab_starts, forcing, density, moving_flags)])

    placed = (
        P("tm", "space", None, None),
        P("tm", None, "space", None, None),
        P("space", None, None),
        P("space", None, None),
    )
    return jax.shard_map(
        local,
        mesh=mesh,
        in_specs=placed,
        out_specs=(P("tm", "space", None, None), P("tm", "space", None, None)),
        check_vma=False,
    )
```

```python
import functools

import jax
import jax.numpy as jnp
from jax import lax
from jax.experimental import pallas as pl
from jax.experimental.pallas import tpu as pltpu
from jax.sharding import PartitionSpec as P

COARSE_SWEEPS = 4
STIFFNESS = 4.0
COARSE_STIFF = 0.25
FORCE_WEIGHT = 0.5
RELAX = 0.8
MASS_FLAG = 3.0

MESH = pl.DeviceIdType.MESH
REACH = COARSE_SWEEPS
SLOTS = 2 * REACH + 1
F32 = jnp.float32
BF16 = jnp.bfloat16


def pieces(x):
    hi = x.astype(BF16).astype(F32)
    rest = x - hi
    mid = rest.astype(BF16).astype(F32)
    low = (rest - mid).astype(BF16).astype(F32)
    return [hi, mid, low]


def kernel(
    n, nt, planes,
    starts, forcing, density, flags, out_starts, out_interior,
    prior, state, came, force, rho, moving, stiff, diag, alpha, beta, local_part,
    ring, own, pair, rows, wide, narrow, spread,
    load_sem, send_sem, recv_sem,
):
    t = lax.axis_index("tm")
    me = lax.axis_index("space")
    ahead, behind = lax.rem(t + 1, nt), lax.rem(t + nt - 1, nt)
    top = planes + 2
    ny, nz = prior.shape[-2:]
    ncy, ncz = 8, nz // 4

    def inside(offset):
        if offset < 0:
            return me >= -offset
        return me < n - offset

    order = [1, -1, 3, -3, 2, -2, 4, -4]
    offsets = [d for d in range(-REACH, REACH + 1)]

    barrier = pltpu.get_barrier_semaphore()
    for d in (1, -1, 2, -2, 3, -3, 4, -4):
        @pl.when(inside(d))
        def _(d=d):
            pl.semaphore_signal(barrier, inc=1, device_id=(t, me + d), device_id_type=MESH)
            pl.semaphore_signal(barrier, inc=1, device_id=(behind, me + d), device_id_type=MESH)
    pl.semaphore_signal(barrier, inc=1, device_id=(behind, me), device_id_type=MESH)

    loads = [
        pltpu.make_async_copy(density, rho, load_sem.at[0]),
        pltpu.make_async_copy(flags, moving, load_sem.at[1]),
        pltpu.make_async_copy(starts.at[0], prior.at[0, pl.ds(2, planes)], load_sem.at[2]),
        pltpu.make_async_copy(forcing.at[0], force, load_sem.at[3]),
    ]
    for load in loads:
        load.start()

    sends = []

    def copy_to(src, dst, k, device):
        return pltpu.make_async_remote_copy(
            src_ref=src, dst_ref=dst, send_sem=send_sem.at[k], recv_sem=recv_sem.at[k],
            device_id=device, device_id_type=MESH,
        )

    def send(src, dst, k, offset, tm):
        copy = copy_to(src, dst, k, (tm, me + offset))
        if offset == 0:
            copy.start()
        else:
            pl.when(inside(offset))(lambda: copy.start())
        sends.append((copy, offset))

    def receive(dst, k, offset):
        copy = copy_to(dst, dst, k, (t, me))
        if offset == 0:
            copy.wait_recv()
        else:
            pl.when(inside(offset))(lambda: copy.wait_recv())

    for d in offsets:
        if d == 0:
            continue

        @pl.when(jnp.logical_not(inside(d)))
        def _(d=d):
            zero = jnp.zeros(own.shape, F32)
            pair[REACH + d, 0] = zero
            pair[REACH + d, 1] = zero
            for step in range(2):
                ring[step, REACH + d] = zero
            if abs(d) == 1:
                side = 0 if d < 0 else 1
                fine_zero = jnp.zeros((ny, nz), F32)
                prior[0, 1 if d < 0 else top] = fine_zero
                local_part[side] = fine_zero
                beta[side * (planes + 1)] = fine_zero
                alpha[0, side * (planes + 1)] = fine_zero
                alpha[1, side * (planes + 1)] = fine_zero
                state[0, side * (top + 1)] = fine_zero
                came[side * (top + 1)] = fine_zero

    narrow[...] = (
        lax.broadcasted_iota(jnp.int32, (nz, ncz), 0) // 4 == lax.broadcasted_iota(jnp.int32, (nz, ncz), 1)
    ).astype(F32).astype(BF16)
    one = (
        lax.broadcasted_iota(jnp.int32, (ncz, nz), 1) // 4 == lax.broadcasted_iota(jnp.int32, (ncz, nz), 0)
    ).astype(F32).astype(BF16)
    for piece in range(3):
        wide[pl.ds(piece * ncz, ncz), :] = one
    rows[...] = jnp.zeros_like(rows)

    row = lax.broadcasted_iota(jnp.int32, (ny, nz), 0)
    lane = lax.broadcasted_iota(jnp.int32, (ny, nz), 1)

    def beside(x):
        up = jnp.where(row == 0, 0.0, pltpu.roll(x, 1, 0))
        down = jnp.where(row == ny - 1, 0.0, pltpu.roll(x, ny - 1, 0))
        left = jnp.where(lane == 0, 0.0, pltpu.roll(x, 1, 1))
        right = jnp.where(lane == nz - 1, 0.0, pltpu.roll(x, nz - 1, 1))
        return (up + down) + (left + right)

    clane = lax.broadcasted_iota(jnp.int32, (ncy, ncz), 1)

    def coarse_beside(x):
        left = jnp.where(clane == 0, 0.0, pltpu.roll(x, 1, 1))
        right = jnp.where(clane == ncz - 1, 0.0, pltpu.roll(x, ncz - 1, 1))
        return (pltpu.roll(x, 1, 0) + pltpu.roll(x, ncy - 1, 0)) + (left + right)

    def coarsen(total, slot):
        stacked = jnp.concatenate(pieces(total), axis=0).astype(BF16)
        product = jnp.dot(stacked, narrow[...], preferred_element_type=F32)
        rows[slot, pl.ds(0, ny), :] = (product[:ny] + product[ny:2 * ny]) + product[2 * ny:]
        parts = [rows[slot, pl.ds(k, ncy, stride=4), :] for k in range(4)]
        return ((parts[0] + parts[1]) + (parts[2] + parts[3])) * (1.0 / 64.0)

    pl.semaphore_wait(barrier, 1 + 2 * sum(inside(d).astype(jnp.int32) for d in offsets if d != 0))
    send(starts.at[0, 0], prior.at[0, top], 1, -1, t)
    send(starts.at[0, planes - 1], prior.at[0, 1], 0, 1, t)

    for load in loads:
        load.wait()

    def coefficients(k):
        conduct = 1.0 / rho[k]
        mass = 1.0 + MASS_FLAG * moving[k].astype(F32)
        full = mass + 6.0 * STIFFNESS * conduct
        relax = RELAX / full
        stiff[k] = STIFFNESS * conduct
        diag[k] = full
        beta[k + 1] = (STIFFNESS * conduct) * relax
        for step in range(2):
            alpha[step, k + 1] = (FORCE_WEIGHT * force[step, k]) * relax
        return mass, conduct

    def smooth(step, i, below=True, above=True):
        here = prior[step, i]
        around = beside(here)
        if below:
            around = around + prior[step, i - 1]
        if above:
            around = around + prior[step, i + 1]
        return here + (alpha[step % 2, i - 1] + beta[i - 1] * (around - 6.0 * here))

    sums = [coefficients(0)]
    send(beta.at[1], beta.at[planes + 1], 3, -1, t)
    part_low = smooth(0, 2, below=False)
    local_part[2] = part_low
    send(local_part.at[2], local_part.at[1], 5, -1, t)
    sums.append(coefficients(planes - 1))
    send(beta.at[planes], beta.at[0], 2, 1, t)
    part_high = smooth(0, planes + 1, above=False)
    local_part[3] = part_high
    send(local_part.at[3], local_part.at[0], 4, 1, t)
    for k in range(1, planes - 1):
        sums.append(coefficients(k))
    for i in range(3, planes + 1):
        state[0, i] = smooth(0, i)
    send(state.at[0, 3], state.at[0, top + 1], 7, -1, t)
    send(state.at[0, planes], state.at[0, 0], 6, 1, t)
    send(alpha.at[1, 1], alpha.at[1, planes + 1], 16, -1, t)
    send(alpha.at[1, planes], alpha.at[1, 0], 15, 1, t)
    mass_sum = functools.reduce(lambda a, b: a + b, [m for m, _ in sums])
    conduct_sum = functools.reduce(lambda a, b: a + b, [c for _, c in sums])

    mass_c = coarsen(mass_sum, 0)
    conduct_c = coarsen(conduct_sum, 1)
    real = lax.broadcasted_iota(jnp.int32, (ncy, ncz), 0) < ny // 4
    relax_c = jnp.where(real, RELAX / jnp.where(real, mass_c + 6.0 * COARSE_STIFF * conduct_c, 1.0), 0.0)
    pair[REACH, 1] = COARSE_STIFF * conduct_c * relax_c

    def residual(step):
        total = jnp.zeros((ny, nz), F32)
        for k in range(planes):
            full, mine = diag[k], state[step, k + 2]
            mass = 1.0 + MASS_FLAG * moving[k].astype(F32)
            around = beside(mine) + (state[step, k + 1] + state[step, k + 3])
            total = total + (mass * prior[step, k + 2] + FORCE_WEIGHT * force[step % 2, k]) - (full * mine - stiff[k] * around)
        return total

    def solve(step, width):
        gam = {i: pair[i, 1] for i in range(1, SLOTS - 1)}
        right = {
            i: pair[i, 0] if step == 0 else ring[step - 1, i] for i in range(1 - width, SLOTS - 1 + width)
        }
        error = right
        for sweep in range(COARSE_SWEEPS - 1):
            reach = COARSE_SWEEPS - 2 - sweep + width
            error = {
                i: (1.0 - RELAX) * error[i] + right[i]
                + gam[i] * (coarse_beside(error[i]) + (error[i - 1] + error[i + 1]))
                for i in range(REACH - reach, REACH + reach + 1)
            }
        return [error[i] for i in range(REACH - width, REACH + width + 1)]

    def expanded(errors):
        for j, error in enumerate(errors):
            for k in range(4):
                spread[j, pl.ds(k, ncy, stride=4), :] = error
        tall = jnp.concatenate([spread[j, pl.ds(0, ny), :] for j in range(len(errors))], axis=0)
        stacked = jnp.concatenate(pieces(tall), axis=1).astype(BF16)
        product = jnp.dot(stacked, wide[...], preferred_element_type=F32)
        return [product[j * ny:(j + 1) * ny] for j in range(len(errors))]

    for step in range(3):
        if step == 0:
            receive(prior.at[0, 1], 0, -1)
            state[0, 2] = local_part[2] + beta[1] * prior[0, 1]
            receive(prior.at[0, top], 1, 1)
            state[0, planes + 1] = local_part[3] + beta[planes] * prior[0, top]
        else:
            for i in range(3, planes + 1):
                state[step, i] = smooth(step, i)
        if step == 1:
            send(state.at[1, 3], came.at[top + 1], 9, -1, ahead)
            send(state.at[1, planes], came.at[0], 8, 1, ahead)
        if step == 0:
            receive(beta.at[0], 2, -1)
            receive(local_part.at[0], 4, -1)
            state[0, 1] = local_part[0] + beta[0] * prior[0, 2]
            receive(beta.at[planes + 1], 3, 1)
            receive(local_part.at[1], 5, 1)
            state[0, top] = local_part[1] + beta[planes + 1] * prior[0, planes + 1]
        else:
            receive(alpha.at[step % 2, 0], 13 + 2 * step, -1)
            receive(alpha.at[step % 2, planes + 1], 14 + 2 * step, 1)
            for i in (1, 2, planes + 1, top):
                state[step, i] = smooth(step, i)
        if step == 1:
            send(state.at[1, pl.ds(1, planes + 2)], came.at[pl.ds(1, planes + 2)], 14, 0, ahead)
        right = relax_c * coarsen(residual(step), step % 2)
        if step == 0:
            pair[REACH, 0] = right
            for d in order:
                send(pair.at[REACH], pair.at[REACH - d], 20 + REACH - d, d, t)
            for d in order:
                receive(pair.at[REACH + d], 20 + REACH + d, d)
            send(alpha.at[0, 1], alpha.at[0, planes + 1], 18, -1, t)
            send(alpha.at[0, planes], alpha.at[0, 0], 17, 1, t)
        elif step == 1:
            own[...] = right
            for d in order + [0]:
                send(own, ring.at[0, REACH - d], 30 + REACH - d, d, ahead)
            for d in order + [0]:
                receive(ring.at[0, REACH + d], 30 + REACH + d, d)
        else:
            ring[1, REACH] = right
            for d in order[:-2]:
                send(ring.at[1, REACH], ring.at[1, REACH - d], 40 + REACH - d, d, t)
            for d in order[:-2]:
                receive(ring.at[1, REACH + d], 40 + REACH + d, d)
        if step < 2:
            corrections = expanded(solve(step, 1))
            if step == 0:
                receive(state.at[0, 0], 6, -1)
                receive(state.at[0, top + 1], 7, 1)
            else:
                receive(came.at[0], 8, -1)
                receive(came.at[top + 1], 9, 1)
                receive(came.at[pl.ds(1, planes + 2)], 14, 0)
            for i in range(planes + 4):
                which = 0 if i < 2 else 2 if i >= top else 1
                base = state[0, i] if step == 0 else came[i]
                prior[step + 1, i] = base + corrections[which]
            if step == 1:
                for k in range(planes):
                    out_starts[0, k] = prior[2, k + 2]
        else:
            correction = expanded(solve(step, 0))[0]
            for k in range(planes):
                out_interior[0, k] = state[2, k + 2] + correction
    for copy, offset in sends:
        if offset == 0:
            copy.wait_send()
        else:
            pl.when(inside(offset))(lambda copy=copy: copy.wait_send())


def solution(mesh):
    n, nt = mesh.shape["space"], mesh.shape["tm"]

    def local(slab_starts, forcing, density, moving_flags):
        _, planes, ny, nz = slab_starts.shape
        block = (planes, ny, nz)
        coarse = (8, nz // 4)
        result = jax.ShapeDtypeStruct(slab_starts.shape, F32)
        return pl.pallas_call(
            functools.partial(kernel, n, nt, planes),
            out_shape=(result, result),
            in_specs=[pl.BlockSpec(memory_space=pl.ANY)] * 4,
            out_specs=(pl.BlockSpec(memory_space=pltpu.VMEM),) * 2,
            scratch_shapes=[
                pltpu.VMEM((3, planes + 4, ny, nz), F32),
                pltpu.VMEM((3, planes + 4, ny, nz), F32),
                pltpu.VMEM((planes + 4, ny, nz), F32),
                pltpu.VMEM((2,) + block, F32),
                pltpu.VMEM(block, F32),
                pltpu.VMEM(block, jnp.int32),
                pltpu.VMEM(block, F32),
                pltpu.VMEM(block, F32),
                pltpu.VMEM((2, planes + 2, ny, nz), F32),
                pltpu.VMEM((planes + 2, ny, nz), F32),
                pltpu.VMEM((4, ny, nz), F32),
                pltpu.VMEM((2, SLOTS) + coarse, F32),
                pltpu.VMEM(coarse, F32),
                pltpu.VMEM((SLOTS, 2) + coarse, F32),
                pltpu.VMEM((2, 32, nz // 4), F32),
                pltpu.VMEM((3 * nz // 4, nz), BF16),
                pltpu.VMEM((nz, nz // 4), BF16),
                pltpu.VMEM((3, 32, nz // 4), F32),
                pltpu.SemaphoreType.DMA((6,)),
                pltpu.SemaphoreType.DMA((60,)),
                pltpu.SemaphoreType.DMA((60,)),
            ],
            compiler_params=pltpu.CompilerParams(
                collective_id=0, has_side_effects=True, vmem_limit_bytes=32 * 1024 * 1024
            ),
            name="cycle",
        )(*[pltpu.with_memory_space_constraint(x, pltpu.HBM) for x in (slab_starts, forcing, density, moving_flags)])

    placed = (
        P("tm", "space", None, None),
        P("tm", None, "space", None, None),
        P("space", None, None),
        P("space", None, None),
    )
    return jax.shard_map(
        local,
        mesh=mesh,
        in_specs=placed,
        out_specs=(P("tm", "space", None, None), P("tm", "space", None, None)),
        check_vma=False,
    )
```

```python
import functools

import jax
import jax.numpy as jnp
from jax import lax
from jax.experimental import pallas as pl
from jax.experimental.pallas import tpu as pltpu
from jax.sharding import PartitionSpec as P

COARSE_SWEEPS = 4
STIFFNESS = 4.0
COARSE_STIFF = 0.25
FORCE_WEIGHT = 0.5
RELAX = 0.8
MASS_FLAG = 3.0

MESH = pl.DeviceIdType.MESH
REACH = COARSE_SWEEPS
SLOTS = 2 * REACH + 1
F32 = jnp.float32
BF16 = jnp.bfloat16


def pieces(x):
    hi = x.astype(BF16).astype(F32)
    rest = x - hi
    mid = rest.astype(BF16).astype(F32)
    low = (rest - mid).astype(BF16).astype(F32)
    return [hi, mid, low]


def kernel(
    n, nt, planes,
    starts, forcing, density, flags, out_starts, out_interior,
    prior, state, came, force, rho, moving, stiff, diag, alpha, beta, local_part,
    ring, own, pair, rows, wide, narrow, spread,
    load_sem, send_sem, recv_sem,
):
    t = lax.axis_index("tm")
    me = lax.axis_index("space")
    ahead, behind = lax.rem(t + 1, nt), lax.rem(t + nt - 1, nt)
    top = planes + 2
    ny, nz = prior.shape[-2:]
    ncy, ncz = 8, nz // 4

    def inside(offset):
        if offset < 0:
            return me >= -offset
        return me < n - offset

    order = [1, -1, 3, -3, 2, -2, 4, -4]
    offsets = [d for d in range(-REACH, REACH + 1)]

    barrier = pltpu.get_barrier_semaphore()
    for d in (1, -1, 2, -2, 3, -3, 4, -4):
        @pl.when(inside(d))
        def _(d=d):
            pl.semaphore_signal(barrier, inc=1, device_id=(t, me + d), device_id_type=MESH)
            pl.semaphore_signal(barrier, inc=1, device_id=(behind, me + d), device_id_type=MESH)
    pl.semaphore_signal(barrier, inc=1, device_id=(behind, me), device_id_type=MESH)

    loads = [
        pltpu.make_async_copy(density, rho, load_sem.at[0]),
        pltpu.make_async_copy(flags, moving, load_sem.at[1]),
        pltpu.make_async_copy(starts.at[0], prior.at[0, pl.ds(2, planes)], load_sem.at[2]),
        pltpu.make_async_copy(forcing.at[0], force, load_sem.at[3]),
    ]
    for load in loads:
        load.start()

    sends = []

    def copy_to(src, dst, k, device):
        return pltpu.make_async_remote_copy(
            src_ref=src, dst_ref=dst, send_sem=send_sem.at[k], recv_sem=recv_sem.at[k],
            device_id=device, device_id_type=MESH,
        )

    def send(src, dst, k, offset, tm):
        copy = copy_to(src, dst, k, (tm, me + offset))
        if offset == 0:
            copy.start()
        else:
            pl.when(inside(offset))(lambda: copy.start())
        sends.append((copy, offset))

    def receive(dst, k, offset):
        copy = copy_to(dst, dst, k, (t, me))
        if offset == 0:
            copy.wait_recv()
        else:
            pl.when(inside(offset))(lambda: copy.wait_recv())

    for d in offsets:
        if d == 0:
            continue

        @pl.when(jnp.logical_not(inside(d)))
        def _(d=d):
            zero = jnp.zeros(own.shape, F32)
            pair[REACH + d, 0] = zero
            pair[REACH + d, 1] = zero
            for step in range(2):
                ring[step, REACH + d] = zero
            if abs(d) == 1:
                side = 0 if d < 0 else 1
                fine_zero = jnp.zeros((ny, nz), F32)
                prior[0, 1 if d < 0 else top] = fine_zero
                local_part[side] = fine_zero
                beta[side * (planes + 1)] = fine_zero
                alpha[0, side * (planes + 1)] = fine_zero
                alpha[1, side * (planes + 1)] = fine_zero
                came[side * (top + 1)] = fine_zero

    narrow[...] = (
        lax.broadcasted_iota(jnp.int32, (nz, ncz), 0) // 4 == lax.broadcasted_iota(jnp.int32, (nz, ncz), 1)
    ).astype(F32).astype(BF16)
    one = (
        lax.broadcasted_iota(jnp.int32, (ncz, nz), 1) // 4 == lax.broadcasted_iota(jnp.int32, (ncz, nz), 0)
    ).astype(F32).astype(BF16)
    for piece in range(3):
        wide[pl.ds(piece * ncz, ncz), :] = one
    rows[...] = jnp.zeros_like(rows)

    row = lax.broadcasted_iota(jnp.int32, (ny, nz), 0)
    lane = lax.broadcasted_iota(jnp.int32, (ny, nz), 1)

    def beside(x):
        up = jnp.where(row == 0, 0.0, pltpu.roll(x, 1, 0))
        down = jnp.where(row == ny - 1, 0.0, pltpu.roll(x, ny - 1, 0))
        left = jnp.where(lane == 0, 0.0, pltpu.roll(x, 1, 1))
        right = jnp.where(lane == nz - 1, 0.0, pltpu.roll(x, nz - 1, 1))
        return (up + down) + (left + right)

    clane = lax.broadcasted_iota(jnp.int32, (ncy, ncz), 1)

    def coarse_beside(x):
        left = jnp.where(clane == 0, 0.0, pltpu.roll(x, 1, 1))
        right = jnp.where(clane == ncz - 1, 0.0, pltpu.roll(x, ncz - 1, 1))
        return (pltpu.roll(x, 1, 0) + pltpu.roll(x, ncy - 1, 0)) + (left + right)

    def coarsen(total, slot):
        stacked = jnp.concatenate(pieces(total), axis=0).astype(BF16)
        product = jnp.dot(stacked, narrow[...], preferred_element_type=F32)
        rows[slot, pl.ds(0, ny), :] = (product[:ny] + product[ny:2 * ny]) + product[2 * ny:]
        parts = [rows[slot, pl.ds(k, ncy, stride=4), :] for k in range(4)]
        return ((parts[0] + parts[1]) + (parts[2] + parts[3])) * (1.0 / 64.0)

    pl.semaphore_wait(barrier, 1 + 2 * sum(inside(d).astype(jnp.int32) for d in offsets if d != 0))
    send(starts.at[0, 0], prior.at[0, top], 1, -1, t)
    send(starts.at[0, planes - 1], prior.at[0, 1], 0, 1, t)

    for load in loads:
        load.wait()

    def coefficients(k):
        conduct = 1.0 / rho[k]
        mass = 1.0 + MASS_FLAG * moving[k].astype(F32)
        full = mass + 6.0 * STIFFNESS * conduct
        relax = RELAX / full
        stiff[k] = STIFFNESS * conduct
        diag[k] = full
        beta[k + 1] = (STIFFNESS * conduct) * relax
        for step in range(2):
            alpha[step, k + 1] = (FORCE_WEIGHT * force[step, k]) * relax
        return mass, conduct

    def smooth(step, i, below=True, above=True):
        here = prior[step, i]
        around = beside(here)
        if below:
            around = around + prior[step, i - 1]
        if above:
            around = around + prior[step, i + 1]
        return here + (alpha[step % 2, i - 1] + beta[i - 1] * (around - 6.0 * here))

    sums = [coefficients(0)]
    send(beta.at[1], beta.at[planes + 1], 3, -1, t)
    part_low = smooth(0, 2, below=False)
    local_part[2] = part_low
    send(local_part.at[2], local_part.at[1], 5, -1, t)
    sums.append(coefficients(planes - 1))
    send(beta.at[planes], beta.at[0], 2, 1, t)
    part_high = smooth(0, planes + 1, above=False)
    local_part[3] = part_high
    send(local_part.at[3], local_part.at[0], 4, 1, t)
    for k in range(1, planes - 1):
        sums.append(coefficients(k))
    for i in range(3, planes + 1):
        state[0, i] = smooth(0, i)
    local_part[4] = alpha[1, 1] + beta[1] * state[0, 3]
    local_part[5] = alpha[1, planes] + beta[planes] * state[0, planes]
    mass_sum = functools.reduce(lambda a, b: a + b, [m for m, _ in sums])
    conduct_sum = functools.reduce(lambda a, b: a + b, [c for _, c in sums])

    mass_c = coarsen(mass_sum, 0)
    conduct_c = coarsen(conduct_sum, 1)
    real = lax.broadcasted_iota(jnp.int32, (ncy, ncz), 0) < ny // 4
    relax_c = jnp.where(real, RELAX / jnp.where(real, mass_c + 6.0 * COARSE_STIFF * conduct_c, 1.0), 0.0)
    pair[REACH, 1] = COARSE_STIFF * conduct_c * relax_c

    def residual(step):
        total = jnp.zeros((ny, nz), F32)
        for k in range(planes):
            full, mine = diag[k], state[step, k + 2]
            mass = 1.0 + MASS_FLAG * moving[k].astype(F32)
            around = beside(mine) + (state[step, k + 1] + state[step, k + 3])
            total = total + (mass * prior[step, k + 2] + FORCE_WEIGHT * force[step % 2, k]) - (full * mine - stiff[k] * around)
        return total

    def solve(step, width):
        gam = {i: pair[i, 1] for i in range(1, SLOTS - 1)}
        right = {
            i: pair[i, 0] if step == 0 else ring[step - 1, i] for i in range(1 - width, SLOTS - 1 + width)
        }
        error = right
        for sweep in range(COARSE_SWEEPS - 1):
            reach = COARSE_SWEEPS - 2 - sweep + width
            error = {
                i: (1.0 - RELAX) * error[i] + right[i]
                + gam[i] * (coarse_beside(error[i]) + (error[i - 1] + error[i + 1]))
                for i in range(REACH - reach, REACH + reach + 1)
            }
        return [error[i] for i in range(REACH - width, REACH + width + 1)]

    def expanded(errors):
        for j, error in enumerate(errors):
            for k in range(4):
                spread[j, pl.ds(k, ncy, stride=4), :] = error
        tall = jnp.concatenate([spread[j, pl.ds(0, ny), :] for j in range(len(errors))], axis=0)
        stacked = jnp.concatenate(pieces(tall), axis=1).astype(BF16)
        product = jnp.dot(stacked, wide[...], preferred_element_type=F32)
        return [product[j * ny:(j + 1) * ny] for j in range(len(errors))]

    for step in range(3):
        if step == 0:
            receive(prior.at[0, 1], 0, -1)
            state[0, 2] = local_part[2] + beta[1] * prior[0, 1]
            receive(prior.at[0, top], 1, 1)
            state[0, planes + 1] = local_part[3] + beta[planes] * prior[0, top]
        else:
            for i in range(3, planes + 1):
                state[step, i] = smooth(step, i)
        if step == 1:
            send(state.at[1, 3], came.at[top + 1], 9, -1, ahead)
            send(state.at[1, planes], came.at[0], 8, 1, ahead)
        if step == 0:
            receive(beta.at[0], 2, -1)
            receive(local_part.at[0], 4, -1)
            state[0, 1] = local_part[0] + beta[0] * prior[0, 2]
            receive(beta.at[planes + 1], 3, 1)
            receive(local_part.at[1], 5, 1)
            state[0, top] = local_part[1] + beta[planes + 1] * prior[0, planes + 1]
        else:
            receive(alpha.at[step % 2, 0], 13 + 2 * step, -1)
            receive(alpha.at[step % 2, planes + 1], 14 + 2 * step, 1)
            for i in (1, 2, planes + 1, top):
                state[step, i] = smooth(step, i)
        if step == 1:
            send(state.at[1, pl.ds(1, planes + 2)], came.at[pl.ds(1, planes + 2)], 14, 0, ahead)
        right = relax_c * coarsen(residual(step), step % 2)
        if step == 0:
            pair[REACH, 0] = right
            for d in order:
                send(pair.at[REACH], pair.at[REACH - d], 20 + REACH - d, d, t)
            send(local_part.at[4], alpha.at[1, planes + 1], 16, -1, t)
            send(local_part.at[5], alpha.at[1, 0], 15, 1, t)
            for d in order:
                receive(pair.at[REACH + d], 20 + REACH + d, d)
            send(alpha.at[0, 1], alpha.at[0, planes + 1], 18, -1, t)
            send(alpha.at[0, planes], alpha.at[0, 0], 17, 1, t)
        elif step == 1:
            own[...] = right
            for d in order + [0]:
                send(own, ring.at[0, REACH - d], 30 + REACH - d, d, ahead)
            for d in order + [0]:
                receive(ring.at[0, REACH + d], 30 + REACH + d, d)
        else:
            ring[1, REACH] = right
            for d in order[:-2]:
                send(ring.at[1, REACH], ring.at[1, REACH - d], 40 + REACH - d, d, t)
            for d in order[:-2]:
                receive(ring.at[1, REACH + d], 40 + REACH + d, d)
        if step < 2:
            corrections = expanded(solve(step, 1))
            if step == 1:
                receive(came.at[0], 8, -1)
                receive(came.at[top + 1], 9, 1)
                receive(came.at[pl.ds(1, planes + 2)], 14, 0)
            for i in range(planes + 4):
                which = 0 if i < 2 else 2 if i >= top else 1
                if step == 0 and i in (0, top + 1):
                    prior[1, i] = corrections[which]
                    continue
                base = state[0, i] if step == 0 else came[i]
                prior[step + 1, i] = base + corrections[which]
            if step == 1:
                for k in range(planes):
                    out_starts[0, k] = prior[2, k + 2]
        else:
            correction = expanded(solve(step, 0))[0]
            for k in range(planes):
                out_interior[0, k] = state[2, k + 2] + correction
    for copy, offset in sends:
        if offset == 0:
            copy.wait_send()
        else:
            pl.when(inside(offset))(lambda copy=copy: copy.wait_send())


def solution(mesh):
    n, nt = mesh.shape["space"], mesh.shape["tm"]

    def local(slab_starts, forcing, density, moving_flags):
        _, planes, ny, nz = slab_starts.shape
        block = (planes, ny, nz)
        coarse = (8, nz // 4)
        result = jax.ShapeDtypeStruct(slab_starts.shape, F32)
        return pl.pallas_call(
            functools.partial(kernel, n, nt, planes),
            out_shape=(result, result),
            in_specs=[pl.BlockSpec(memory_space=pl.ANY)] * 4,
            out_specs=(pl.BlockSpec(memory_space=pltpu.VMEM),) * 2,
            scratch_shapes=[
                pltpu.VMEM((3, planes + 4, ny, nz), F32),
                pltpu.VMEM((3, planes + 4, ny, nz), F32),
                pltpu.VMEM((planes + 4, ny, nz), F32),
                pltpu.VMEM((2,) + block, F32),
                pltpu.VMEM(block, F32),
                pltpu.VMEM(block, jnp.int32),
                pltpu.VMEM(block, F32),
                pltpu.VMEM(block, F32),
                pltpu.VMEM((2, planes + 2, ny, nz), F32),
                pltpu.VMEM((planes + 2, ny, nz), F32),
                pltpu.VMEM((6, ny, nz), F32),
                pltpu.VMEM((2, SLOTS) + coarse, F32),
                pltpu.VMEM(coarse, F32),
                pltpu.VMEM((SLOTS, 2) + coarse, F32),
                pltpu.VMEM((2, 32, nz // 4), F32),
                pltpu.VMEM((3 * nz // 4, nz), BF16),
                pltpu.VMEM((nz, nz // 4), BF16),
                pltpu.VMEM((3, 32, nz // 4), F32),
                pltpu.SemaphoreType.DMA((6,)),
                pltpu.SemaphoreType.DMA((60,)),
                pltpu.SemaphoreType.DMA((60,)),
            ],
            compiler_params=pltpu.CompilerParams(
                collective_id=0, has_side_effects=True, vmem_limit_bytes=32 * 1024 * 1024
            ),
            name="cycle",
        )(*[pltpu.with_memory_space_constraint(x, pltpu.HBM) for x in (slab_starts, forcing, density, moving_flags)])

    placed = (
        P("tm", "space", None, None),
        P("tm", None, "space", None, None),
        P("space", None, None),
        P("space", None, None),
    )
    return jax.shard_map(
        local,
        mesh=mesh,
        in_specs=placed,
        out_specs=(P("tm", "space", None, None), P("tm", "space", None, None)),
        check_vma=False,
    )
```

```python
import functools

import jax
import jax.numpy as jnp
from jax import lax
from jax.experimental import pallas as pl
from jax.experimental.pallas import tpu as pltpu
from jax.sharding import PartitionSpec as P

COARSE_SWEEPS = 4
STIFFNESS = 4.0
COARSE_STIFF = 0.25
FORCE_WEIGHT = 0.5
RELAX = 0.8
MASS_FLAG = 3.0

MESH = pl.DeviceIdType.MESH
REACH = COARSE_SWEEPS
SLOTS = 2 * REACH + 1
F32 = jnp.float32
BF16 = jnp.bfloat16


def pieces(x):
    hi = x.astype(BF16).astype(F32)
    rest = x - hi
    mid = rest.astype(BF16).astype(F32)
    low = (rest - mid).astype(BF16).astype(F32)
    return [hi, mid, low]


def kernel(
    n, nt, planes,
    starts, forcing, density, flags, out_starts, out_interior,
    prior, state, came, force, rho, moving, stiff, diag, alpha, beta, local_part,
    ring, own, pair, rows, wide, narrow, spread,
    load_sem, send_sem, recv_sem,
):
    t = lax.axis_index("tm")
    me = lax.axis_index("space")
    ahead, behind = lax.rem(t + 1, nt), lax.rem(t + nt - 1, nt)
    half = lax.rem(t, 2)
    mate = t + 1 - 2 * half
    top = planes + 2
    ny, nz = prior.shape[-2:]
    ncy, ncz = 8, nz // 4
    mine = pl.ds(pl.multiple_of(half * (nz // 2), nz // 2), nz // 2)
    theirs = pl.ds(pl.multiple_of((1 - half) * (nz // 2), nz // 2), nz // 2)

    def inside(offset):
        if offset < 0:
            return me >= -offset
        return me < n - offset

    order = [1, -1, 3, -3, 2, -2, 4, -4]
    offsets = [d for d in range(-REACH, REACH + 1)]

    barrier = pltpu.get_barrier_semaphore()
    for d in (1, -1, 2, -2, 3, -3, 4, -4):
        @pl.when(inside(d))
        def _(d=d):
            pl.semaphore_signal(barrier, inc=1, device_id=(t, me + d), device_id_type=MESH)
            pl.semaphore_signal(barrier, inc=1, device_id=(behind, me + d), device_id_type=MESH)
    pl.semaphore_signal(barrier, inc=1, device_id=(behind, me), device_id_type=MESH)
    pl.semaphore_signal(barrier, inc=1, device_id=(ahead, me), device_id_type=MESH)

    loads = [
        pltpu.make_async_copy(density, rho, load_sem.at[0]),
        pltpu.make_async_copy(flags, moving, load_sem.at[1]),
        pltpu.make_async_copy(starts.at[0], prior.at[0, pl.ds(2, planes)], load_sem.at[2]),
        pltpu.make_async_copy(forcing.at[0], force, load_sem.at[3]),
    ]
    for load in loads:
        load.start()

    sends = []

    def copy_to(src, dst, k, device):
        return pltpu.make_async_remote_copy(
            src_ref=src, dst_ref=dst, send_sem=send_sem.at[k], recv_sem=recv_sem.at[k],
            device_id=device, device_id_type=MESH,
        )

    def send(src, dst, k, offset, tm):
        copy = copy_to(src, dst, k, (tm, me + offset))
        if offset == 0:
            copy.start()
        else:
            pl.when(inside(offset))(lambda: copy.start())
        sends.append((copy, offset))

    def pass_on(part, k, offset):
        copy = copy_to(part, part, k, (mate, me))
        pl.when(inside(offset))(lambda: copy.start())
        sends.append((copy, offset))

    def receive(dst, k, offset):
        copy = copy_to(dst, dst, k, (t, me))
        if offset == 0:
            copy.wait_recv()
        else:
            pl.when(inside(offset))(lambda: copy.wait_recv())

    for d in offsets:
        if d == 0:
            continue

        @pl.when(jnp.logical_not(inside(d)))
        def _(d=d):
            zero = jnp.zeros(own.shape, F32)
            pair[REACH + d, 0] = zero
            pair[REACH + d, 1] = zero
            for step in range(2):
                ring[step, REACH + d] = zero
            if abs(d) == 1:
                side = 0 if d < 0 else 1
                fine_zero = jnp.zeros((ny, nz), F32)
                prior[0, 1 if d < 0 else top] = fine_zero
                local_part[side] = fine_zero
                beta[side * (planes + 1)] = fine_zero
                alpha[0, side * (planes + 1)] = fine_zero
                alpha[1, side * (planes + 1)] = fine_zero
                came[side * (top + 1)] = fine_zero

    narrow[...] = (
        lax.broadcasted_iota(jnp.int32, (nz, ncz), 0) // 4 == lax.broadcasted_iota(jnp.int32, (nz, ncz), 1)
    ).astype(F32).astype(BF16)
    one = (
        lax.broadcasted_iota(jnp.int32, (ncz, nz), 1) // 4 == lax.broadcasted_iota(jnp.int32, (ncz, nz), 0)
    ).astype(F32).astype(BF16)
    for piece in range(3):
        wide[pl.ds(piece * ncz, ncz), :] = one
    rows[...] = jnp.zeros_like(rows)

    row = lax.broadcasted_iota(jnp.int32, (ny, nz), 0)
    lane = lax.broadcasted_iota(jnp.int32, (ny, nz), 1)

    def beside(x):
        up = jnp.where(row == 0, 0.0, pltpu.roll(x, 1, 0))
        down = jnp.where(row == ny - 1, 0.0, pltpu.roll(x, ny - 1, 0))
        left = jnp.where(lane == 0, 0.0, pltpu.roll(x, 1, 1))
        right = jnp.where(lane == nz - 1, 0.0, pltpu.roll(x, nz - 1, 1))
        return (up + down) + (left + right)

    clane = lax.broadcasted_iota(jnp.int32, (ncy, ncz), 1)

    def coarse_beside(x):
        left = jnp.where(clane == 0, 0.0, pltpu.roll(x, 1, 1))
        right = jnp.where(clane == ncz - 1, 0.0, pltpu.roll(x, ncz - 1, 1))
        return (pltpu.roll(x, 1, 0) + pltpu.roll(x, ncy - 1, 0)) + (left + right)

    def coarsen(total, slot):
        stacked = jnp.concatenate(pieces(total), axis=0).astype(BF16)
        product = jnp.dot(stacked, narrow[...], preferred_element_type=F32)
        rows[slot, pl.ds(0, ny), :] = (product[:ny] + product[ny:2 * ny]) + product[2 * ny:]
        parts = [rows[slot, pl.ds(k, ncy, stride=4), :] for k in range(4)]
        return ((parts[0] + parts[1]) + (parts[2] + parts[3])) * (1.0 / 64.0)

    pl.semaphore_wait(barrier, 2 + 2 * sum(inside(d).astype(jnp.int32) for d in offsets if d != 0))

    for load in loads:
        load.wait()

    def coefficients(k):
        conduct = 1.0 / rho[k]
        mass = 1.0 + MASS_FLAG * moving[k].astype(F32)
        full = mass + 6.0 * STIFFNESS * conduct
        relax = RELAX / full
        stiff[k] = STIFFNESS * conduct
        diag[k] = full
        beta[k + 1] = (STIFFNESS * conduct) * relax
        for step in range(2):
            alpha[step, k + 1] = (FORCE_WEIGHT * force[step, k]) * relax
        return mass, conduct

    def smooth(step, i, below=True, above=True):
        here = prior[step, i]
        around = beside(here)
        if below:
            around = around + prior[step, i - 1]
        if above:
            around = around + prior[step, i + 1]
        return here + (alpha[step % 2, i - 1] + beta[i - 1] * (around - 6.0 * here))

    sums = [coefficients(0)]
    send(beta.at[1, :, mine], beta.at[planes + 1, :, mine], 3, -1, t)
    sums.append(coefficients(planes - 1))
    send(beta.at[planes, :, mine], beta.at[0, :, mine], 2, 1, t)
    send(starts.at[0, 0], prior.at[0, top], 1, -1, t)
    send(starts.at[0, planes - 1], prior.at[0, 1], 0, 1, t)
    part_low = smooth(0, 2, below=False)
    local_part[2] = part_low
    send(local_part.at[2], local_part.at[1], 5, -1, t)
    part_high = smooth(0, planes + 1, above=False)
    local_part[3] = part_high
    send(local_part.at[3], local_part.at[0], 4, 1, t)
    for k in range(1, planes - 1):
        sums.append(coefficients(k))
    for i in range(3, planes + 1):
        state[0, i] = smooth(0, i)
    local_part[4] = alpha[1, 1] + beta[1] * state[0, 3]
    local_part[5] = alpha[1, planes] + beta[planes] * state[0, planes]
    mass_sum = functools.reduce(lambda a, b: a + b, [m for m, _ in sums])
    conduct_sum = functools.reduce(lambda a, b: a + b, [c for _, c in sums])

    mass_c = coarsen(mass_sum, 0)
    conduct_c = coarsen(conduct_sum, 1)
    real = lax.broadcasted_iota(jnp.int32, (ncy, ncz), 0) < ny // 4
    relax_c = jnp.where(real, RELAX / jnp.where(real, mass_c + 6.0 * COARSE_STIFF * conduct_c, 1.0), 0.0)
    pair[REACH, 1] = COARSE_STIFF * conduct_c * relax_c

    def residual(step):
        total = jnp.zeros((ny, nz), F32)
        for k in range(planes):
            full, mine = diag[k], state[step, k + 2]
            mass = 1.0 + MASS_FLAG * moving[k].astype(F32)
            around = beside(mine) + (state[step, k + 1] + state[step, k + 3])
            total = total + (mass * prior[step, k + 2] + FORCE_WEIGHT * force[step % 2, k]) - (full * mine - stiff[k] * around)
        return total

    def solve(step, width):
        gam = {i: pair[i, 1] for i in range(1, SLOTS - 1)}
        right = {
            i: pair[i, 0] if step == 0 else ring[step - 1, i] for i in range(1 - width, SLOTS - 1 + width)
        }
        error = right
        for sweep in range(COARSE_SWEEPS - 1):
            reach = COARSE_SWEEPS - 2 - sweep + width
            error = {
                i: (1.0 - RELAX) * error[i] + right[i]
                + gam[i] * (coarse_beside(error[i]) + (error[i - 1] + error[i + 1]))
                for i in range(REACH - reach, REACH + reach + 1)
            }
        return [error[i] for i in range(REACH - width, REACH + width + 1)]

    def expanded(errors):
        for j, error in enumerate(errors):
            for k in range(4):
                spread[j, pl.ds(k, ncy, stride=4), :] = error
        tall = jnp.concatenate([spread[j, pl.ds(0, ny), :] for j in range(len(errors))], axis=0)
        stacked = jnp.concatenate(pieces(tall), axis=1).astype(BF16)
        product = jnp.dot(stacked, wide[...], preferred_element_type=F32)
        return [product[j * ny:(j + 1) * ny] for j in range(len(errors))]

    for step in range(3):
        if step == 0:
            receive(beta.at[0, :, mine], 2, -1)
            pass_on(beta.at[0, :, mine], 6, -1)
            receive(beta.at[planes + 1, :, mine], 3, 1)
            pass_on(beta.at[planes + 1, :, mine], 7, 1)
            receive(prior.at[0, 1], 0, -1)
            state[0, 2] = local_part[2] + beta[1] * prior[0, 1]
            receive(prior.at[0, top], 1, 1)
            state[0, planes + 1] = local_part[3] + beta[planes] * prior[0, top]
        else:
            for i in range(3, planes + 1):
                state[step, i] = smooth(step, i)
        if step == 1:
            send(state.at[1, 3], came.at[top + 1], 9, -1, ahead)
            send(state.at[1, planes], came.at[0], 8, 1, ahead)
        if step == 0:
            receive(beta.at[0, :, theirs], 6, -1)
            receive(local_part.at[0], 4, -1)
            state[0, 1] = local_part[0] + beta[0] * prior[0, 2]
            receive(beta.at[planes + 1, :, theirs], 7, 1)
            receive(local_part.at[1], 5, 1)
            state[0, top] = local_part[1] + beta[planes + 1] * prior[0, planes + 1]
        else:
            receive(alpha.at[step % 2, 0], 13 + 2 * step, -1)
            receive(alpha.at[step % 2, planes + 1], 14 + 2 * step, 1)
            for i in (1, 2, planes + 1, top):
                state[step, i] = smooth(step, i)
        if step == 1:
            send(state.at[1, pl.ds(1, planes + 2)], came.at[pl.ds(1, planes + 2)], 14, 0, ahead)
        right = relax_c * coarsen(residual(step), step % 2)
        if step == 0:
            pair[REACH, 0] = right
            for d in order:
                send(pair.at[REACH], pair.at[REACH - d], 20 + REACH - d, d, t)
            send(local_part.at[4], alpha.at[1, planes + 1], 16, -1, t)
            send(local_part.at[5], alpha.at[1, 0], 15, 1, t)
            for d in order:
                receive(pair.at[REACH + d], 20 + REACH + d, d)
            send(alpha.at[0, 1], alpha.at[0, planes + 1], 18, -1, t)
            send(alpha.at[0, planes], alpha.at[0, 0], 17, 1, t)
        elif step == 1:
            own[...] = right
            for d in order + [0]:
                send(own, ring.at[0, REACH - d], 30 + REACH - d, d, ahead)
            for d in order + [0]:
                receive(ring.at[0, REACH + d], 30 + REACH + d, d)
        else:
            ring[1, REACH] = right
            for d in order[:-2]:
                send(ring.at[1, REACH], ring.at[1, REACH - d], 40 + REACH - d, d, t)
            for d in order[:-2]:
                receive(ring.at[1, REACH + d], 40 + REACH + d, d)
        if step < 2:
            corrections = expanded(solve(step, 1))
            if step == 1:
                receive(came.at[0], 8, -1)
                receive(came.at[top + 1], 9, 1)
                receive(came.at[pl.ds(1, planes + 2)], 14, 0)
            for i in range(planes + 4):
                which = 0 if i < 2 else 2 if i >= top else 1
                if step == 0 and i in (0, top + 1):
                    prior[1, i] = corrections[which]
                    continue
                base = state[0, i] if step == 0 else came[i]
                prior[step + 1, i] = base + corrections[which]
            if step == 1:
                for k in range(planes):
                    out_starts[0, k] = prior[2, k + 2]
        else:
            correction = expanded(solve(step, 0))[0]
            for k in range(planes):
                out_interior[0, k] = state[2, k + 2] + correction
    for copy, offset in sends:
        if offset == 0:
            copy.wait_send()
        else:
            pl.when(inside(offset))(lambda copy=copy: copy.wait_send())


def solution(mesh):
    n, nt = mesh.shape["space"], mesh.shape["tm"]

    def local(slab_starts, forcing, density, moving_flags):
        _, planes, ny, nz = slab_starts.shape
        block = (planes, ny, nz)
        coarse = (8, nz // 4)
        result = jax.ShapeDtypeStruct(slab_starts.shape, F32)
        return pl.pallas_call(
            functools.partial(kernel, n, nt, planes),
            out_shape=(result, result),
            in_specs=[pl.BlockSpec(memory_space=pl.ANY)] * 4,
            out_specs=(pl.BlockSpec(memory_space=pltpu.VMEM),) * 2,
            scratch_shapes=[
                pltpu.VMEM((3, planes + 4, ny, nz), F32),
                pltpu.VMEM((3, planes + 4, ny, nz), F32),
                pltpu.VMEM((planes + 4, ny, nz), F32),
                pltpu.VMEM((2,) + block, F32),
                pltpu.VMEM(block, F32),
                pltpu.VMEM(block, jnp.int32),
                pltpu.VMEM(block, F32),
                pltpu.VMEM(block, F32),
                pltpu.VMEM((2, planes + 2, ny, nz), F32),
                pltpu.VMEM((planes + 2, ny, nz), F32),
                pltpu.VMEM((6, ny, nz), F32),
                pltpu.VMEM((2, SLOTS) + coarse, F32),
                pltpu.VMEM(coarse, F32),
                pltpu.VMEM((SLOTS, 2) + coarse, F32),
                pltpu.VMEM((2, 32, nz // 4), F32),
                pltpu.VMEM((3 * nz // 4, nz), BF16),
                pltpu.VMEM((nz, nz // 4), BF16),
                pltpu.VMEM((3, 32, nz // 4), F32),
                pltpu.SemaphoreType.DMA((6,)),
                pltpu.SemaphoreType.DMA((60,)),
                pltpu.SemaphoreType.DMA((60,)),
            ],
            compiler_params=pltpu.CompilerParams(
                collective_id=0, has_side_effects=True, vmem_limit_bytes=32 * 1024 * 1024
            ),
            name="cycle",
        )(*[pltpu.with_memory_space_constraint(x, pltpu.HBM) for x in (slab_starts, forcing, density, moving_flags)])

    placed = (
        P("tm", "space", None, None),
        P("tm", None, "space", None, None),
        P("space", None, None),
        P("space", None, None),
    )
    return jax.shard_map(
        local,
        mesh=mesh,
        in_specs=placed,
        out_specs=(P("tm", "space", None, None), P("tm", "space", None, None)),
        check_vma=False,
    )
```

```python
import functools

import jax
import jax.numpy as jnp
from jax import lax
from jax.experimental import pallas as pl
from jax.experimental.pallas import tpu as pltpu
from jax.sharding import PartitionSpec as P

COARSE_SWEEPS = 4
STIFFNESS = 4.0
COARSE_STIFF = 0.25
FORCE_WEIGHT = 0.5
RELAX = 0.8
MASS_FLAG = 3.0

MESH = pl.DeviceIdType.MESH
REACH = COARSE_SWEEPS
SLOTS = 2 * REACH + 1
F32 = jnp.float32
BF16 = jnp.bfloat16


def pieces(x):
    hi = x.astype(BF16).astype(F32)
    rest = x - hi
    mid = rest.astype(BF16).astype(F32)
    low = (rest - mid).astype(BF16).astype(F32)
    return [hi, mid, low]


def kernel(
    n, nt, planes,
    starts, forcing, density, flags, out_starts, out_interior,
    prior, state, came, force, rho, moving, stiff, diag, alpha, beta, local_part,
    ring, own, pair, rows, wide, narrow, spread,
    load_sem, send_sem, recv_sem,
):
    t = lax.axis_index("tm")
    me = lax.axis_index("space")
    ahead, behind = lax.rem(t + 1, nt), lax.rem(t + nt - 1, nt)
    half = lax.rem(t, 2)
    mate = t + 1 - 2 * half
    top = planes + 2
    ny, nz = prior.shape[-2:]
    ncy, ncz = 8, nz // 4
    mine = pl.ds(pl.multiple_of(half * (nz // 2), nz // 2), nz // 2)
    theirs = pl.ds(pl.multiple_of((1 - half) * (nz // 2), nz // 2), nz // 2)

    def inside(offset):
        if offset < 0:
            return me >= -offset
        return me < n - offset

    order = [1, -1, 3, -3, 2, -2, 4, -4]
    offsets = [d for d in range(-REACH, REACH + 1)]

    barrier = pltpu.get_barrier_semaphore()
    for d in (1, -1, 2, -2, 3, -3, 4, -4):
        @pl.when(inside(d))
        def _(d=d):
            pl.semaphore_signal(barrier, inc=1, device_id=(t, me + d), device_id_type=MESH)
            pl.semaphore_signal(barrier, inc=1, device_id=(behind, me + d), device_id_type=MESH)
    pl.semaphore_signal(barrier, inc=1, device_id=(behind, me), device_id_type=MESH)
    pl.semaphore_signal(barrier, inc=1, device_id=(ahead, me), device_id_type=MESH)

    loads = [
        pltpu.make_async_copy(density, rho, load_sem.at[0]),
        pltpu.make_async_copy(flags, moving, load_sem.at[1]),
        pltpu.make_async_copy(starts.at[0], prior.at[0, pl.ds(2, planes)], load_sem.at[2]),
        pltpu.make_async_copy(forcing.at[0], force, load_sem.at[3]),
    ]
    for load in loads:
        load.start()

    sends = []

    def copy_to(src, dst, k, device):
        return pltpu.make_async_remote_copy(
            src_ref=src, dst_ref=dst, send_sem=send_sem.at[k], recv_sem=recv_sem.at[k],
            device_id=device, device_id_type=MESH,
        )

    def send(src, dst, k, offset, tm):
        copy = copy_to(src, dst, k, (tm, me + offset))
        if offset == 0:
            copy.start()
        else:
            pl.when(inside(offset))(lambda: copy.start())
        sends.append((copy, offset))

    def pass_on(part, k, offset):
        copy = copy_to(part, part, k, (mate, me))
        pl.when(inside(offset))(lambda: copy.start())
        sends.append((copy, offset))

    def receive(dst, k, offset):
        copy = copy_to(dst, dst, k, (t, me))
        if offset == 0:
            copy.wait_recv()
        else:
            pl.when(inside(offset))(lambda: copy.wait_recv())

    for d in offsets:
        if d == 0:
            continue

        @pl.when(jnp.logical_not(inside(d)))
        def _(d=d):
            zero = jnp.zeros(own.shape, F32)
            pair[REACH + d, 0] = zero
            pair[REACH + d, 1] = zero
            for step in range(2):
                ring[step, REACH + d] = zero
            if abs(d) == 1:
                side = 0 if d < 0 else 1
                fine_zero = jnp.zeros((ny, nz), F32)
                prior[0, 1 if d < 0 else top] = fine_zero
                local_part[side] = fine_zero
                beta[side * (planes + 1)] = fine_zero
                alpha[0, side * (planes + 1)] = fine_zero
                alpha[1, side * (planes + 1)] = fine_zero
                came[side * (top + 1)] = fine_zero

    narrow[...] = (
        lax.broadcasted_iota(jnp.int32, (nz, ncz), 0) // 4 == lax.broadcasted_iota(jnp.int32, (nz, ncz), 1)
    ).astype(F32).astype(BF16)
    one = (
        lax.broadcasted_iota(jnp.int32, (ncz, nz), 1) // 4 == lax.broadcasted_iota(jnp.int32, (ncz, nz), 0)
    ).astype(F32).astype(BF16)
    for piece in range(3):
        wide[pl.ds(piece * ncz, ncz), :] = one
    rows[...] = jnp.zeros_like(rows)

    row = lax.broadcasted_iota(jnp.int32, (ny, nz), 0)
    lane = lax.broadcasted_iota(jnp.int32, (ny, nz), 1)

    def beside(x):
        up = jnp.where(row == 0, 0.0, pltpu.roll(x, 1, 0))
        down = jnp.where(row == ny - 1, 0.0, pltpu.roll(x, ny - 1, 0))
        left = jnp.where(lane == 0, 0.0, pltpu.roll(x, 1, 1))
        right = jnp.where(lane == nz - 1, 0.0, pltpu.roll(x, nz - 1, 1))
        return (up + down) + (left + right)

    clane = lax.broadcasted_iota(jnp.int32, (ncy, ncz), 1)

    def coarse_beside(x):
        left = jnp.where(clane == 0, 0.0, pltpu.roll(x, 1, 1))
        right = jnp.where(clane == ncz - 1, 0.0, pltpu.roll(x, ncz - 1, 1))
        return (pltpu.roll(x, 1, 0) + pltpu.roll(x, ncy - 1, 0)) + (left + right)

    def coarsen(total, slot):
        stacked = jnp.concatenate(pieces(total), axis=0).astype(BF16)
        product = jnp.dot(stacked, narrow[...], preferred_element_type=F32)
        rows[slot, pl.ds(0, ny), :] = (product[:ny] + product[ny:2 * ny]) + product[2 * ny:]
        parts = [rows[slot, pl.ds(k, ncy, stride=4), :] for k in range(4)]
        return ((parts[0] + parts[1]) + (parts[2] + parts[3])) * (1.0 / 64.0)

    pl.semaphore_wait(barrier, 2 + 2 * sum(inside(d).astype(jnp.int32) for d in offsets if d != 0))

    for load in loads:
        load.wait()

    def coefficients(k):
        conduct = 1.0 / rho[k]
        mass = 1.0 + MASS_FLAG * moving[k].astype(F32)
        full = mass + 6.0 * STIFFNESS * conduct
        relax = RELAX / full
        stiff[k] = STIFFNESS * conduct
        diag[k] = full
        beta[k + 1] = (STIFFNESS * conduct) * relax
        for step in range(2):
            alpha[step, k + 1] = (FORCE_WEIGHT * force[step, k]) * relax
        return mass, conduct

    def smooth(step, i, below=True, above=True):
        here = prior[step, i]
        around = beside(here)
        if below:
            around = around + prior[step, i - 1]
        if above:
            around = around + prior[step, i + 1]
        return here + (alpha[step % 2, i - 1] + beta[i - 1] * (around - 6.0 * here))

    sums = [coefficients(0)]
    send(beta.at[1, :, mine], beta.at[planes + 1, :, mine], 3, -1, t)
    sums.append(coefficients(planes - 1))
    send(beta.at[planes, :, mine], beta.at[0, :, mine], 2, 1, t)
    send(starts.at[0, 0], prior.at[0, top], 1, -1, t)
    send(starts.at[0, planes - 1], prior.at[0, 1], 0, 1, t)
    part_low = smooth(0, 2, below=False)
    local_part[2] = part_low
    send(local_part.at[2], local_part.at[1], 5, -1, t)
    part_high = smooth(0, planes + 1, above=False)
    local_part[3] = part_high
    send(local_part.at[3], local_part.at[0], 4, 1, t)
    for k in range(1, planes - 1):
        sums.append(coefficients(k))
    for i in range(3, planes + 1):
        state[0, i] = smooth(0, i)
    local_part[4] = alpha[1, 1] + beta[1] * state[0, 3]
    local_part[5] = alpha[1, planes] + beta[planes] * state[0, planes]
    mass_sum = functools.reduce(lambda a, b: a + b, [m for m, _ in sums])
    conduct_sum = functools.reduce(lambda a, b: a + b, [c for _, c in sums])

    mass_c = coarsen(mass_sum, 0)
    conduct_c = coarsen(conduct_sum, 1)
    real = lax.broadcasted_iota(jnp.int32, (ncy, ncz), 0) < ny // 4
    relax_c = jnp.where(real, RELAX / jnp.where(real, mass_c + 6.0 * COARSE_STIFF * conduct_c, 1.0), 0.0)
    pair[REACH, 1] = COARSE_STIFF * conduct_c * relax_c

    def residual(step):
        total = jnp.zeros((ny, nz), F32)
        for k in range(planes):
            full, mine = diag[k], state[step, k + 2]
            mass = 1.0 + MASS_FLAG * moving[k].astype(F32)
            around = beside(mine) + (state[step, k + 1] + state[step, k + 3])
            total = total + (mass * prior[step, k + 2] + FORCE_WEIGHT * force[step % 2, k]) - (full * mine - stiff[k] * around)
        return total

    def solve(step, width):
        gam = {i: pair[i, 1] for i in range(1, SLOTS - 1)}
        right = {
            i: pair[i, 0] if step == 0 else ring[step - 1, i] for i in range(1 - width, SLOTS - 1 + width)
        }
        error = right
        for sweep in range(COARSE_SWEEPS - 1):
            reach = COARSE_SWEEPS - 2 - sweep + width
            error = {
                i: (1.0 - RELAX) * error[i] + right[i]
                + gam[i] * (coarse_beside(error[i]) + (error[i - 1] + error[i + 1]))
                for i in range(REACH - reach, REACH + reach + 1)
            }
        return [error[i] for i in range(REACH - width, REACH + width + 1)]

    def expanded(errors):
        for j, error in enumerate(errors):
            for k in range(4):
                spread[j, pl.ds(k, ncy, stride=4), :] = error
        tall = jnp.concatenate([spread[j, pl.ds(0, ny), :] for j in range(len(errors))], axis=0)
        stacked = jnp.concatenate(pieces(tall), axis=1).astype(BF16)
        product = jnp.dot(stacked, wide[...], preferred_element_type=F32)
        return [product[j * ny:(j + 1) * ny] for j in range(len(errors))]

    for step in range(3):
        if step == 0:
            receive(beta.at[0, :, mine], 2, -1)
            pass_on(beta.at[0, :, mine], 6, -1)
            receive(beta.at[planes + 1, :, mine], 3, 1)
            pass_on(beta.at[planes + 1, :, mine], 7, 1)
            receive(prior.at[0, 1], 0, -1)
            state[0, 2] = local_part[2] + beta[1] * prior[0, 1]
            receive(prior.at[0, top], 1, 1)
            state[0, planes + 1] = local_part[3] + beta[planes] * prior[0, top]
        else:
            for i in range(3, planes + 1):
                state[step, i] = smooth(step, i)
        if step == 1:
            send(state.at[1, 3], came.at[top + 1], 9, -1, ahead)
            send(state.at[1, planes], came.at[0], 8, 1, ahead)
        if step == 0:
            receive(beta.at[0, :, theirs], 6, -1)
            receive(local_part.at[0], 4, -1)
            state[0, 1] = local_part[0] + beta[0] * prior[0, 2]
            receive(beta.at[planes + 1, :, theirs], 7, 1)
            receive(local_part.at[1], 5, 1)
            state[0, top] = local_part[1] + beta[planes + 1] * prior[0, planes + 1]
        else:
            receive(alpha.at[step % 2, 0], 13 + 2 * step, -1)
            receive(alpha.at[step % 2, planes + 1], 14 + 2 * step, 1)
            for i in (1, 2, planes + 1, top):
                state[step, i] = smooth(step, i)
        if step == 1:
            send(state.at[1, pl.ds(1, planes + 2)], came.at[pl.ds(1, planes + 2)], 14, 0, ahead)
        right = relax_c * coarsen(residual(step), step % 2)
        if step == 0:
            pair[REACH, 0] = right
            for d in order:
                send(pair.at[REACH], pair.at[REACH - d], 20 + REACH - d, d, t)
            send(local_part.at[4], alpha.at[1, planes + 1], 16, -1, t)
            send(local_part.at[5], alpha.at[1, 0], 15, 1, t)
            for d in order:
                receive(pair.at[REACH + d], 20 + REACH + d, d)
        elif step == 1:
            own[...] = right
            for d in order + [0]:
                send(own, ring.at[0, REACH - d], 30 + REACH - d, d, ahead)
            send(alpha.at[0, 1], alpha.at[0, planes + 1], 18, -1, t)
            send(alpha.at[0, planes], alpha.at[0, 0], 17, 1, t)
            for d in order + [0]:
                receive(ring.at[0, REACH + d], 30 + REACH + d, d)
        else:
            ring[1, REACH] = right
            for d in order[:-2]:
                send(ring.at[1, REACH], ring.at[1, REACH - d], 40 + REACH - d, d, t)
            for d in order[:-2]:
                receive(ring.at[1, REACH + d], 40 + REACH + d, d)
        if step < 2:
            corrections = expanded(solve(step, 1))
            if step == 1:
                receive(came.at[0], 8, -1)
                receive(came.at[top + 1], 9, 1)
                receive(came.at[pl.ds(1, planes + 2)], 14, 0)
            for i in range(planes + 4):
                which = 0 if i < 2 else 2 if i >= top else 1
                if step == 0 and i in (0, top + 1):
                    prior[1, i] = corrections[which]
                    continue
                base = state[0, i] if step == 0 else came[i]
                prior[step + 1, i] = base + corrections[which]
            if step == 1:
                for k in range(planes):
                    out_starts[0, k] = prior[2, k + 2]
        else:
            correction = expanded(solve(step, 0))[0]
            for k in range(planes):
                out_interior[0, k] = state[2, k + 2] + correction
    for copy, offset in sends:
        if offset == 0:
            copy.wait_send()
        else:
            pl.when(inside(offset))(lambda copy=copy: copy.wait_send())


def solution(mesh):
    n, nt = mesh.shape["space"], mesh.shape["tm"]

    def local(slab_starts, forcing, density, moving_flags):
        _, planes, ny, nz = slab_starts.shape
        block = (planes, ny, nz)
        coarse = (8, nz // 4)
        result = jax.ShapeDtypeStruct(slab_starts.shape, F32)
        return pl.pallas_call(
            functools.partial(kernel, n, nt, planes),
            out_shape=(result, result),
            in_specs=[pl.BlockSpec(memory_space=pl.ANY)] * 4,
            out_specs=(pl.BlockSpec(memory_space=pltpu.VMEM),) * 2,
            scratch_shapes=[
                pltpu.VMEM((3, planes + 4, ny, nz), F32),
                pltpu.VMEM((3, planes + 4, ny, nz), F32),
                pltpu.VMEM((planes + 4, ny, nz), F32),
                pltpu.VMEM((2,) + block, F32),
                pltpu.VMEM(block, F32),
                pltpu.VMEM(block, jnp.int32),
                pltpu.VMEM(block, F32),
                pltpu.VMEM(block, F32),
                pltpu.VMEM((2, planes + 2, ny, nz), F32),
                pltpu.VMEM((planes + 2, ny, nz), F32),
                pltpu.VMEM((6, ny, nz), F32),
                pltpu.VMEM((2, SLOTS) + coarse, F32),
                pltpu.VMEM(coarse, F32),
                pltpu.VMEM((SLOTS, 2) + coarse, F32),
                pltpu.VMEM((2, 32, nz // 4), F32),
                pltpu.VMEM((3 * nz // 4, nz), BF16),
                pltpu.VMEM((nz, nz // 4), BF16),
                pltpu.VMEM((3, 32, nz // 4), F32),
                pltpu.SemaphoreType.DMA((6,)),
                pltpu.SemaphoreType.DMA((60,)),
                pltpu.SemaphoreType.DMA((60,)),
            ],
            compiler_params=pltpu.CompilerParams(
                collective_id=0, has_side_effects=True, vmem_limit_bytes=32 * 1024 * 1024
            ),
            name="cycle",
        )(*[pltpu.with_memory_space_constraint(x, pltpu.HBM) for x in (slab_starts, forcing, density, moving_flags)])

    placed = (
        P("tm", "space", None, None),
        P("tm", None, "space", None, None),
        P("space", None, None),
        P("space", None, None),
    )
    return jax.shard_map(
        local,
        mesh=mesh,
        in_specs=placed,
        out_specs=(P("tm", "space", None, None), P("tm", "space", None, None)),
        check_vma=False,
    )
```
